512 devices in a mesh: dp: 64 (over z, x), feat: 8 (over y, core).
Axes of the slice: x: 4, y: 4, z: 16, core: 2. Of those that a mesh axis runs over, the one named last changes fastest.
Arguments:
- grads: bfloat16 [8, 32768, 4, 128], P('feat', 'dp'), may hold values from -6 to 6
- block_ids: int32 [8, 32768, 4], P('feat', 'dp'), may hold values from 0 to 127, all different within a row; in each aligned block of 512 rows (0 to 511, 512 to 1023, ..., all dimensions but the last counted through in order) at most 24 rows name the same one
- probe: bfloat16 [128, 8, 128, 512], P('dp', 'feat'), may hold values from -0.09375 to 0.09375
Outputs:
- whitened: float32 [32768, 512], P(('dp', 'feat'))
The draws below stay inside these ranges and needn't reach their ends.
Inputs may be any that keep to these rules, and one draw needn't show every extreme that they name: block_ids[j, s, k] is a local block number in slice j; the ids of one sample in one slice are distinct; among the 512 samples of one index of dp, no number appears more than 24 times in one slice, and some number appears exactly 24 times.
All inputs are finite; a program needn't handle non-finite values.
Results may differ from the reference program's by a relative error of at most 0.012.
Values may be sent and summed in bfloat16 or wider, within the bound.
A program may use at most 64 MiB of HBM per device.

```python
import math
import jax
import jax.numpy as jnp
import numpy as np
from jax import lax

BW = 128
RANK = 512
K_J = 4
S_DEV = 512
SLICES = 8
SAMPLES = 32768
BF = 128
MOST = 24
KTOT = 32


def steps_of(own_key, extent, shards, smallest, largest):
    level, own = 1.0, jax.random.fold_in(own_key, 6)
    for axis_at, parts in shards:
        draws = jnp.exp(jax.random.uniform(jax.random.fold_in(own, axis_at), (parts,), jnp.float32, smallest / len(shards), largest / len(shards)))
        level = level * jnp.repeat(draws, extent[axis_at] // parts).reshape([-1 if axis == axis_at else 1 for axis in range(len(extent))])
    return level


def assign_block(own_key, own, number, rows, count, top, most, lean):
    ranking = jax.random.permutation(own_key, count)
    heavy_load, ordinary = portions_of(count, rows * top, most, lean, True), portions_of(count, rows * top, most, lean, False)
    places = jnp.arange(count)

    def named(tallies, turn):
        used = int((tallies > 0).sum())
        fixed = max(1, used // 4)
        moved = fixed + (places - fixed + turn * (used - fixed)) % max(1, count - fixed)
        return jnp.zeros((count,), jnp.int32).at[ranking[jnp.where(places < fixed, places, moved)]].set(jnp.asarray(tallies, jnp.int32))

    tallies = jnp.where(number % 4 == 0, named(heavy_load, number // 4), named(ordinary, number - number // 4 - 1))
    mixed = jax.random.permutation(jax.random.fold_in(own, 3), count)
    source_of, sink = mixed[0:count // 2 * 2:2], mixed[1:count // 2 * 2:2]
    slack = jnp.minimum(tallies[source_of] - 1, most - tallies[sink]) // 2
    slack = jnp.where((source_of == ranking[0]) | (sink == ranking[0]) | (tallies[sink] == 0), 0, jnp.maximum(slack, 0))
    moved = jax.random.randint(jax.random.fold_in(own, 4), (count // 2,), 0, 1 << 20) % (slack + 1)
    tallies = tallies.at[source_of].add(-moved).at[sink].add(moved)
    labels = jnp.searchsorted(jnp.cumsum(tallies), jnp.arange(rows * top), side="right").astype(jnp.int32)
    grid = labels.reshape(top, rows).T
    grid = grid[jax.random.permutation(jax.random.fold_in(own, 1), rows)]
    turn = jax.random.randint(jax.random.fold_in(own, 2), (rows, 1), 0, top)
    return jnp.take_along_axis(grid, (jnp.arange(top)[None, :] + turn) % top, axis=1)


def portions_of(count, total, most, skew, full):
    weights = [(1 << 20) // math.isqrt(grade ** skew) + 1 for grade in range(1, count + 1)]
    largest = most if full else min(most, max(-(-total // count), total * weights[0] // sum(weights)))
    least = 1 if total - largest >= count - 1 else 0
    given, spare = [largest] + [least] * (count - 1), total - largest - least * (count - 1)
    while spare > 0:
        movable = [i for i in range(1, count) if given[i] < largest] or [i for i in range(1, count) if given[i] < most]
        whole, left = sum([weights[i] for i in movable]), spare
        for i in movable:
            extra = min(most - given[i], max(1, left * weights[i] // whole), spare)
            given[i] = given[i] + extra
            spare = spare - extra
    return np.array(given)


def gaussian(key, shape, deviation, bound, cuts=(), kind=jnp.bfloat16):
    values = deviation * jax.random.normal(key, shape, jnp.float32)
    if cuts:
        values = values * steps_of(key, shape, cuts, -0.22, 0.18)
    return jnp.clip(values, -bound, bound).astype(kind)


def setup_inputs(seed: int = 0) -> dict:
    arg_keys = jax.random.split(jax.random.key(seed), 4)
    grads = gaussian(arg_keys[0], (SLICES, SAMPLES, K_J, BW), 1.0, 6.0, ((0, 8), (1, 64)))
    block_ids_keys = jax.random.split(jax.random.fold_in(arg_keys[1], 1), SLICES * SAMPLES // S_DEV)
    block_ids_turns = jax.random.permutation(jax.random.fold_in(arg_keys[1], 3), SLICES * SAMPLES // S_DEV)
    block_ids = jax.vmap(lambda own, number: assign_block(jax.random.fold_in(arg_keys[1], 2), own, number, S_DEV, BF, K_J, MOST, 2))(block_ids_keys, block_ids_turns).reshape((SLICES, SAMPLES, K_J))
    probe = gaussian(arg_keys[2], (BF, SLICES, BW, RANK), (KTOT * BW) ** -0.5, 0.09375, ((0, 64), (1, 8)))
    return {"grads": grads, "block_ids": block_ids, "probe": probe}


root_steps = 4

def inverse_root(gram):
    width = gram.shape[0]
    ident = jnp.eye(width, dtype=jnp.float32)
    scale = jnp.trace(gram) / width
    current = gram / scale
    result = ident
    for step in range(root_steps):
        middle = 1.5 * ident - 0.5 * jnp.dot(result, current, precision=lax.Precision.HIGHEST)
        if step + 1 < root_steps:
            current = jnp.dot(current, middle, precision=lax.Precision.HIGHEST)
        result = jnp.dot(middle, result, precision=lax.Precision.HIGHEST)
    return result / jnp.sqrt(scale)

def reference(grads, block_ids, probe):
    slices = grads.shape[0]
    samples = grads.shape[1]
    group = 8
    g_blocks = grads.reshape(slices, samples // group, group, K_J, BW).transpose(1, 0, 2, 3, 4)
    i_blocks = block_ids.reshape(slices, samples // group, group, K_J).transpose(1, 0, 2, 3)
    slice_index = jnp.arange(slices, dtype=jnp.int32)[:, None, None]

    def one_group(pair):
        values, ids = pair
        rows = probe[ids, slice_index]
        prod = jnp.einsum('jskb,jskbr->jskr', values.astype(jnp.float32), rows.astype(jnp.float32))
        prod = prod.astype(jnp.bfloat16)
        return lax.optimization_barrier(jnp.sum(prod.astype(jnp.float32), axis=(0, 2)))
    sketch_sum = lax.map(one_group, (g_blocks, i_blocks)).reshape(samples, RANK)
    sketch = sketch_sum.astype(jnp.bfloat16)
    gram = lax.dot_general(sketch, sketch, (((0,), (0,)), ((), ())), preferred_element_type=jnp.float32)
    gram = gram + 0.1 * samples * jnp.eye(RANK, dtype=jnp.float32)
    root = inverse_root(gram)
    return math.sqrt(samples) * jnp.dot(sketch.astype(jnp.float32), root, precision=lax.Precision.HIGHEST)
```

```python
import math

import jax
import jax.numpy as jnp
from jax import lax
from jax.experimental import pallas as pl
from jax.experimental.pallas import tpu as pltpu
from jax.sharding import PartitionSpec as P

ridge = 0.1
root_steps = 4
NX = 4
NC = 2
MESH = pl.DeviceIdType.MESH
bf16, f32 = jnp.bfloat16, jnp.float32


def sizes():
    return lax.axis_size("dp") // NX, lax.axis_size("feat") // NC


class Place:
    def __init__(self, nz, ny):
        dp, feat = lax.axis_index("dp"), lax.axis_index("feat")
        self.nz, self.ny = nz, ny
        self.z, self.x = dp // NX, lax.rem(dp, NX)
        self.y, self.c = feat // NC, lax.rem(feat, NC)

    def at(self, dz=0, dx=0, dy=0, dc=0):
        z = lax.rem(self.z + (dz % self.nz), self.nz)
        x = lax.rem(self.x + (dx % NX), NX)
        y = lax.rem(self.y + (dy % self.ny), self.ny)
        c = lax.rem(self.c + dc, NC)
        return {"dp": z * NX + x, "feat": y * NC + c}


def greet(others):
    barrier = pltpu.get_barrier_semaphore()
    for other in others:
        pl.semaphore_signal(barrier, inc=1, device_id=other, device_id_type=MESH)
    pl.semaphore_wait(barrier, len(others))


def sketch_kernel(
    nz, ny, ge, probe, out,
    gx, codes, dense, pbuf, acc, csend, crecv, xs, xo, xr, rows, ys, yr,
    zss, zrs, xss, xrs, css, crs, oss, ors, qss, qrs, yss, yrs,
):
    here = Place(nz, ny)
    z, x, y, c = here.z, here.x, here.y, here.c
    s_dev, s_ext = 512, ge.shape[0]
    cut = 272
    right_z, left_z = here.at(dz=1), here.at(dz=-1)
    right_x, left_x = here.at(dx=1), here.at(dx=-1)
    other_core = here.at(dc=1)
    greet([right_z, left_z, right_x, left_x, other_core] + [here.at(dy=d) for d in range(1, ny)])

    def remote(src, dst, ssem, rsem, to):
        return pltpu.make_async_remote_copy(
            src_ref=src, dst_ref=dst, send_sem=ssem, recv_sem=rsem, device_id=to, device_id_type=MESH
        )

    half = nz // 2
    started = []

    def go(copy):
        copy.start()
        started.append(copy)

    def zcopy(way, h, s, w):
        src, dst = (s, s + 1) if way == 0 else ((nz - s) % nz, nz - 1 - s)
        part = pl.ds(128 * w, 128)
        return remote(
            pbuf.at[h, src, part], pbuf.at[h, dst, part], zss.at[way, h, s, w], zrs.at[way, h, s, w],
            right_z if way == 0 else left_z,
        )

    def zsent(way, s, w):
        return s < half - 1 or (s == half - 1 and w == way)

    def arrive(h, s):
        for w in range(2):
            for way in range(2):
                if zsent(way, s, w):
                    zcopy(way, h, s, w).wait_recv()
                    if s + 1 < half and zsent(way, s + 1, w):
                        go(zcopy(way, h, s + 1, w))

    def own(h):
        for w in range(2):
            for way in range(2):
                go(zcopy(way, h, 0, w))

    lo, hi = pl.ds(0, cut), pl.ds(cut, s_ext - cut)
    xc = {
        "ra": remote(ge.at[lo], gx.at[0, lo], xss.at[0], xrs.at[0], right_x),
        "rb": remote(ge.at[hi], gx.at[0, hi], xss.at[1], xrs.at[1], right_x),
        "lb": remote(ge.at[hi], gx.at[1, hi], xss.at[2], xrs.at[2], left_x),
        "la": remote(ge.at[lo], gx.at[1, lo], xss.at[3], xrs.at[3], left_x),
        "fa": remote(gx.at[0, lo], gx.at[2, lo], xss.at[4], xrs.at[4], right_x),
        "fb": remote(gx.at[1, hi], gx.at[2, hi], xss.at[5], xrs.at[5], left_x),
    }

    def expand(t):
        src = ge if t == 0 else gx.at[t - 1]
        ids = src[pl.ds(s_dev, 16), :].astype(jnp.int32)
        m = lax.rem(z + nz - ids // 8, nz)
        code = jnp.where(lax.rem(ids // 2, NX) == x, 2 * m + lax.rem(ids, 2), 255).astype(f32).astype(bf16)
        picks = (
            lax.broadcasted_iota(jnp.int32, (16, 512), 0) == lax.broadcasted_iota(jnp.int32, (16, 512), 1) // 128
        ).astype(f32).astype(bf16)
        codes[...] = lax.dot_general(
            code, picks, (((0,), (0,)), ((), ())), preferred_element_type=f32
        ).astype(bf16)

        @pl.loop(0, s_dev // 32)
        def _(i):
            r = pl.ds(pl.multiple_of(i * 32, 32), 32)
            g = [src[r, pl.ds(128 * k, 128)] for k in range(4)]
            q = [codes[r, pl.ds(128 * k, 128)] for k in range(4)]
            for b in range(2 * nz):
                v = jnp.zeros_like(g[0])
                for k in range(4):
                    v = jnp.where(q[k] == jnp.asarray(b, bf16), g[k], v)
                dense[t, r, pl.ds(128 * b, 128)] = v

    def product(h, t, spans, first):
        total = None
        for lo_m, hi_m in spans:
            depth = (hi_m - lo_m) * 256
            term = jnp.dot(
                dense[t, :, pl.ds(lo_m * 256, depth)], pbuf[h, lo_m:hi_m].reshape(depth, 256),
                preferred_element_type=f32,
            )
            total = term if total is None else total + term
        if not first:
            total = total + acc[h, t]
        acc[h, t] = total

    def ccopy(h, t):
        return remote(csend.at[h, t], crecv.at[h, t], css.at[h, t], crs.at[h, t], other_core)

    def give_core(h, t):
        for yy in range(ny):
            csend[h, t, yy] = acc[h, t, pl.ds(pl.multiple_of(128 * yy + 64 * (1 - c), 64), 64), :].astype(bf16)
        go(ccopy(h, t))

    def both(h, t, yy):
        mine = acc[h, t, pl.ds(pl.multiple_of(128 * yy + 64 * c, 64), 64), :]
        return mine + crecv[h, t, yy].astype(f32)

    top, bottom = pl.ds(0, ny // 2), pl.ds(ny // 2, ny // 2)
    tops, bottoms = range(ny // 2), range(ny // 2, ny)

    def ocopy(h, way):
        part = top if way == 0 else bottom
        return remote(
            xs.at[h, 2, part], xo.at[h, way], oss.at[h, way], ors.at[h, way], right_x if way == 0 else left_x
        )

    def qcopy(h, way, part):
        span = top if part == 0 else bottom
        return remote(
            xs.at[h, 1 - way, span], xr.at[h, way, span], qss.at[h, way, part], qrs.at[h, way, part],
            right_x if way == 0 else left_x,
        )

    def ycopy(h, d):
        return remote(ys.at[h, d - 1], yr.at[h, d - 1], yss.at[h, d - 1], yrs.at[h, d - 1], here.at(dy=d))

    def far(h):
        ccopy(h, 3).wait_recv()
        for yy in range(ny):
            xs[h, 2, yy] = both(h, 3, yy).astype(bf16)
        go(ocopy(h, 0))
        go(ocopy(h, 1))

    def near(h):
        ccopy(h, 2).wait_recv()
        for yy in bottoms:
            xs[h, 1, yy] = both(h, 2, yy).astype(bf16)
        go(qcopy(h, 0, 1))
        ccopy(h, 1).wait_recv()
        for yy in tops:
            xs[h, 0, yy] = both(h, 1, yy).astype(bf16)
        go(qcopy(h, 1, 0))

    def joined(h):
        ocopy(h, 0).wait_recv()
        for yy in tops:
            xs[h, 1, yy] = (both(h, 2, yy) + xo[h, 0, yy].astype(f32)).astype(bf16)
        go(qcopy(h, 0, 0))
        ocopy(h, 1).wait_recv()
        for yy in bottoms:
            xs[h, 0, yy] = (both(h, 1, yy) + xo[h, 1, yy - ny // 2].astype(f32)).astype(bf16)
        go(qcopy(h, 1, 1))

    def home(h):
        ccopy(h, 0).wait_recv()
        for way in range(2):
            for part in range(2):
                qcopy(h, way, part).wait_recv()
        for yy in range(ny):
            rows[h, yy] = both(h, 0, yy) + xr[h, 0, yy].astype(f32) + xr[h, 1, yy].astype(f32)
        for d in range(1, ny):
            ys[h, d - 1] = rows[h, lax.rem(y + d, ny)].astype(bf16)
            go(ycopy(h, d))

    def finish(h):
        total = rows[h, y]
        for d in range(1, ny):
            ycopy(h, d).wait_recv()
            total = total + yr[h, d - 1].astype(f32)
        out[:, pl.ds(256 * h, 256)] = total.astype(bf16)

    for h in range(2):
        pbuf[h, 0] = probe[:, pl.ds(256 * h, 256)]
    own(0)
    for name in ("ra", "lb", "rb", "la"):
        go(xc[name])
    expand(0)
    whole = [(0, nz)]
    early, late = [(0, 6), (11, nz)], [(6, 11)]
    for s in range(half):
        arrive(0, s)
        if s == 1:
            xc["ra"].wait_recv()
            go(xc["fa"])
            xc["lb"].wait_recv()
            go(xc["fb"])
        if s == 3:
            xc["rb"].wait_recv()
            expand(1)
        if s == 4:
            xc["la"].wait_recv()
            expand(2)
        if s == half - 2:
            own(1)
    xc["fa"].wait_recv()
    xc["fb"].wait_recv()
    expand(3)
    for s in range(half):
        if s == half - 1:
            product(1, 0, early, True)
        arrive(1, s)
        if s < 4:
            product(0, 3 - s, whole, True)
            give_core(0, 3 - s)
        if s == 2:
            far(0)
        if s == 3:
            near(0)
        if s == 4:
            joined(0)
            home(0)
        if s == 5:
            finish(0)
            product(1, 3, early, True)
        if s == 6:
            product(1, 2, early, True)
            product(1, 1, early, True)
    for t in (3, 2, 1, 0):
        product(1, t, late, False)
        give_core(1, t)
        if t == 2:
            far(1)
        if t == 0:
            near(1)
    joined(1)
    home(1)
    finish(1)
    for copy in started:
        copy.wait_send()


def sketch_rows(grads, block_ids, probe):
    nz, ny = sizes()
    s_dev = grads.shape[1]
    values = grads[0].reshape(s_dev, 512)
    ids = jnp.pad(block_ids[0].T.astype(f32).astype(bf16), ((0, 12), (0, 0)))
    ge = jnp.concatenate([values, ids], axis=0)
    blocks = probe.reshape(256, 512)
    half = nz // 2
    dma = pltpu.SemaphoreType.DMA
    return pl.pallas_call(
        lambda *refs: sketch_kernel(nz, ny, *refs),
        out_shape=jax.ShapeDtypeStruct((64, 512), bf16),
        in_specs=[pl.BlockSpec(memory_space=pltpu.VMEM)] * 2,
        out_specs=pl.BlockSpec(memory_space=pltpu.VMEM),
        scratch_shapes=[
            pltpu.VMEM((3, s_dev + 16, 512), bf16),
            pltpu.VMEM((s_dev, 512), bf16),
            pltpu.VMEM((4, s_dev, nz * 256), bf16),
            pltpu.VMEM((2, nz, 256, 256), bf16),
            pltpu.VMEM((2, 4, s_dev, 256), f32),
            pltpu.VMEM((2, 4, ny, 64, 256), bf16),
            pltpu.VMEM((2, 4, ny, 64, 256), bf16),
            pltpu.VMEM((2, 3, ny, 64, 256), bf16),
            pltpu.VMEM((2, 2, ny // 2, 64, 256), bf16),
            pltpu.VMEM((2, 2, ny, 64, 256), bf16),
            pltpu.VMEM((2, ny, 64, 256), f32),
            pltpu.VMEM((2, ny - 1, 64, 256), bf16),
            pltpu.VMEM((2, ny - 1, 64, 256), bf16),
            dma((2, 2, half, 2)), dma((2, 2, half, 2)),
            dma((6,)), dma((6,)),
            dma((2, 4)), dma((2, 4)),
            dma((2, 2)), dma((2, 2)),
            dma((2, 2, 2)), dma((2, 2, 2)),
            dma((2, ny - 1)), dma((2, ny - 1)),
        ],
        compiler_params=pltpu.CompilerParams(
            collective_id=0, has_side_effects=True, vmem_limit_bytes=56 << 20
        ),
        name="sketch",
    )(ge, blocks)


def pieces(value):
    hi = value.astype(bf16)
    return hi, (value - hi.astype(f32)).astype(bf16)


def times(a, b):
    (ah, al), (bh, bl) = a, b
    total = jnp.dot(ah, bh, preferred_element_type=f32) + jnp.dot(ah, bl, preferred_element_type=f32)
    return total + jnp.dot(al, bh, preferred_element_type=f32)


def whiten_kernel(
    nz, ny, samples, s_ref, out,
    sy, gram, gsend, gr, zsend, zr, zall, xall, yall, whole,
    yss, yrs, rss, rrs, zss, zrs, ass, ars, bss, brs, dss, drs, ess, ers,
):
    here = Place(nz, ny)
    z, x, y, c = here.z, here.x, here.y, here.c
    cx = [(dx, dc) for dx in range(NX) for dc in range(NC)][1:]
    ydev = {d: here.at(dy=d) for d in range(1, ny)}
    cxdev = {p: here.at(dx=p[0], dc=p[1]) for p in cx}
    zdev = {d: here.at(dz=d) for d in range(1, nz)}
    greet(list(ydev.values()) + list(cxdev.values()) + list(zdev.values()))
    started = []

    def remote(src, dst, ssem, rsem, to):
        return pltpu.make_async_remote_copy(
            src_ref=src, dst_ref=dst, send_sem=ssem, recv_sem=rsem, device_id=to, device_id_type=MESH
        )

    def go(copy):
        copy.start()
        started.append(copy)

    mine = s_ref[...]
    sy[0] = mine
    ys = [remote(sy.at[0], sy.at[d], yss.at[d - 1], yrs.at[d - 1], ydev[d]) for d in range(1, ny)]
    for copy in ys:
        go(copy)
    for copy in ys:
        copy.wait_recv()
    rows = ny * 64
    right = sy[...].reshape(rows, 512)
    left = sy[:, :, pl.ds(pl.multiple_of(128 * y, 128), 128)].reshape(rows, 128)
    gram[...] = lax.dot_general(left, right, (((0,), (0,)), ((), ())), preferred_element_type=f32)
    copies = []
    for n, (dx, dc) in enumerate(cx):
        at = 64 * lax.rem(c + dc, NC) + 16 * lax.rem(x + dx, NX)
        copies.append(
            remote(
                gram.at[pl.ds(pl.multiple_of(at, 16), 16)], gr.at[n], rss.at[n], rrs.at[n], cxdev[(dx, dc)]
            )
        )
        go(copies[-1])
    part = gram[pl.ds(pl.multiple_of(64 * c + 16 * x, 16), 16), :]
    for n, copy in enumerate(copies):
        copy.wait_recv()
        part = part + gr[n]
    for i in range(4):
        for j in range(4):
            zsend[4 * i + j] = part[4 * i : 4 * i + 4, 128 * j : 128 * j + 128]
    copies = []
    for d in range(1, nz):
        copies.append(
            remote(zsend.at[lax.rem(z + d, nz)], zr.at[d - 1], zss.at[d - 1], zrs.at[d - 1], zdev[d])
        )
        go(copies[-1])
    total = zsend[z]
    for d, copy in enumerate(copies):
        copy.wait_recv()
        total = total + zr[d]
    zall[z] = total
    copies = [remote(zall.at[z], zall.at[z], ass.at[d - 1], ars.at[d - 1], zdev[d]) for d in range(1, nz)]
    for copy in copies:
        go(copy)
    for d in range(1, nz):
        remote(
            zall.at[z], zall.at[lax.rem(z + nz - d, nz)], ass.at[d - 1], ars.at[d - 1], zdev[d]
        ).wait_recv()
    xall[x] = zall[...]
    copies = [remote(xall.at[x], xall.at[x], bss.at[d - 1], brs.at[d - 1], here.at(dx=d)) for d in range(1, NX)]
    for copy in copies:
        go(copy)
    for d in range(1, NX):
        remote(
            xall.at[x], xall.at[lax.rem(x + NX - d, NX)], bss.at[d - 1], brs.at[d - 1], here.at(dx=d)
        ).wait_recv()
    yall[y, c] = xall[...]
    copies = [remote(yall.at[y, c], yall.at[y, c], dss.at[d - 1], drs.at[d - 1], ydev[d]) for d in range(1, ny)]
    for copy in copies:
        go(copy)
    other = cxdev[(0, 1)]
    go(remote(yall.at[y, c], yall.at[y, c], ess.at[0], ers.at[0], other))
    for d in range(1, ny):
        from_y = lax.rem(y + ny - d, ny)
        remote(yall.at[y, c], yall.at[from_y, c], dss.at[d - 1], drs.at[d - 1], ydev[d]).wait_recv()
        go(remote(yall.at[from_y, c], yall.at[from_y, c], ess.at[d], ers.at[d], other))
    for d in range(ny):
        from_y = lax.rem(y + ny - d, ny)
        remote(yall.at[y, c], yall.at[from_y, 1 - c], ess.at[d], ers.at[d], other).wait_recv()
    for yy in range(ny):
        for cc in range(NC):
            for xx in range(NX):
                at = 128 * yy + 64 * cc + 16 * xx
                for i in range(4):
                    for j in range(4):
                        whole[at + 4 * i : at + 4 * i + 4, 128 * j : 128 * j + 128] = yall[yy, cc, xx, 4 * i + j]
    width = whole.shape[0]
    diag = lax.broadcasted_iota(jnp.int32, (width, width), 0) == lax.broadcasted_iota(jnp.int32, (width, width), 1)
    g = whole[...]
    g = jnp.where(diag, g + ridge * samples, g)
    scale = jnp.sum(jnp.where(diag, g, 0.0), keepdims=True) * (1.0 / width)
    w = g / scale
    v = mine.astype(f32)
    for step in range(root_steps):
        m = jnp.where(diag, 1.5 - 0.5 * w, -0.5 * w)
        mp = pieces(m)
        v = times(pieces(v), mp)
        if step + 1 < root_steps:
            w = times(pieces(times(pieces(w), mp)), mp)
    out[...] = v * (math.sqrt(samples) / jnp.sqrt(scale))
    for copy in started:
        copy.wait_send()


def whitened(sketch):
    nz, ny = sizes()
    samples = 512 * nz * NX
    dma = pltpu.SemaphoreType.DMA
    vmem = pltpu.VMEM
    n = NX * NC - 1
    return pl.pallas_call(
        lambda *refs: whiten_kernel(nz, ny, samples, *refs),
        out_shape=jax.ShapeDtypeStruct((64, 512), f32),
        in_specs=[pl.BlockSpec(memory_space=pltpu.VMEM)],
        out_specs=pl.BlockSpec(memory_space=pltpu.VMEM),
        scratch_shapes=[
            vmem((ny, 64, 512), bf16),
            vmem((128, 512), f32),
            vmem((16, 512), f32),
            vmem((n, 16, 512), f32),
            vmem((nz, 4, 128), f32),
            vmem((nz - 1, 4, 128), f32),
            vmem((nz, 4, 128), f32),
            vmem((NX, nz, 4, 128), f32),
            vmem((ny, NC, NX, nz, 4, 128), f32),
            vmem((512, 512), f32),
            dma((ny - 1,)), dma((ny - 1,)),
            dma((n,)), dma((n,)),
            dma((nz - 1,)), dma((nz - 1,)),
            dma((nz - 1,)), dma((nz - 1,)),
            dma((NX - 1,)), dma((NX - 1,)),
            dma((ny - 1,)), dma((ny - 1,)),
            dma((ny,)), dma((ny,)),
        ],
        compiler_params=pltpu.CompilerParams(
            collective_id=1, has_side_effects=True, vmem_limit_bytes=48 << 20
        ),
        name="whiten",
    )(sketch)


def local(grads, block_ids, probe):
    return whitened(sketch_rows(grads, block_ids, probe))


def solution(mesh):
    return jax.shard_map(
        local,
        mesh=mesh,
        in_specs=(P("feat", "dp", None, None), P("feat", "dp", None), P("dp", "feat", None, None)),
        out_specs=P(("dp", "feat"), None),
        check_vma=False,
    )
```

```python
import math

import jax
import jax.numpy as jnp
from jax import lax
from jax.experimental import pallas as pl
from jax.experimental.pallas import tpu as pltpu
from jax.sharding import PartitionSpec as P

ridge = 0.1
root_steps = 4
NX = 4
NC = 2
MESH = pl.DeviceIdType.MESH
bf16, f32 = jnp.bfloat16, jnp.float32


def sizes():
    return lax.axis_size("dp") // NX, lax.axis_size("feat") // NC


class Place:
    def __init__(self, nz, ny):
        dp, feat = lax.axis_index("dp"), lax.axis_index("feat")
        self.nz, self.ny = nz, ny
        self.z, self.x = dp // NX, lax.rem(dp, NX)
        self.y, self.c = feat // NC, lax.rem(feat, NC)

    def at(self, dz=0, dx=0, dy=0, dc=0):
        z = lax.rem(self.z + (dz % self.nz), self.nz)
        x = lax.rem(self.x + (dx % NX), NX)
        y = lax.rem(self.y + (dy % self.ny), self.ny)
        c = lax.rem(self.c + dc, NC)
        return {"dp": z * NX + x, "feat": y * NC + c}


def pieces(value):
    hi = value.astype(bf16)
    return hi, (value - hi.astype(f32)).astype(bf16)


def times(a, b):
    (ah, al), (bh, bl) = a, b
    total = jnp.dot(ah, bh, preferred_element_type=f32) + jnp.dot(ah, bl, preferred_element_type=f32)
    return total + jnp.dot(al, bh, preferred_element_type=f32)


def kernel(
    nz, ny, samples, grads, ids, probe, out,
    ge, gx, codes, dense, pbuf, acc, csend, crecv, xs, xo, xr, rows, ys, yr,
    sy, gram, gr, zsend, zr, zall, xall, yall, whole,
    zss, zrs, xss, xrs, css, crs, oss, ors, qss, qrs, yss, yrs,
    sss, srs, rss, rrs, ess, ers, fss, frs, ass, ars, bss, brs, dss, drs,
):
    here = Place(nz, ny)
    z, x, y, c = here.z, here.x, here.y, here.c
    s_dev, s_ext = 512, ge.shape[0]
    cut = 272
    right_z, left_z = here.at(dz=1), here.at(dz=-1)
    right_x, left_x = here.at(dx=1), here.at(dx=-1)
    other_core = here.at(dc=1)
    ydev = {d: here.at(dy=d) for d in range(1, ny)}
    near = [right_z, left_z, right_x, left_x, other_core] + list(ydev.values())
    barrier = pltpu.get_barrier_semaphore()
    for other in near:
        pl.semaphore_signal(barrier, inc=1, device_id=other, device_id_type=MESH)

    for h in range(2):
        pbuf[h, 0] = probe[:, pl.ds(256 * h, 256)]
    row = lax.broadcasted_iota(jnp.int32, (256, 256), 0)
    picked = 4 * lax.rem(row, 64) + row // 64 == lax.broadcasted_iota(jnp.int32, (256, 256), 1)
    pick = picked.astype(f32).astype(bf16)
    for i in range(s_dev // 64):
        part = jnp.dot(pick, grads[256 * i : 256 * i + 256], preferred_element_type=f32).astype(bf16)
        for k in range(4):
            ge[64 * i : 64 * i + 64, 128 * k : 128 * k + 128] = part[64 * k : 64 * k + 64]
    ge[s_dev:, :] = jnp.concatenate([ids[...].astype(f32), jnp.zeros((12, s_dev), f32)], axis=0).astype(bf16)
    pl.semaphore_wait(barrier, len(near))

    def remote(src, dst, ssem, rsem, to):
        return pltpu.make_async_remote_copy(
            src_ref=src, dst_ref=dst, send_sem=ssem, recv_sem=rsem, device_id=to, device_id_type=MESH
        )

    half = nz // 2
    started = []

    def go(copy):
        copy.start()
        started.append(copy)

    def zcopy(way, h, s, w):
        src, dst = (s, s + 1) if way == 0 else ((nz - s) % nz, nz - 1 - s)
        part = pl.ds(128 * w, 128)
        return remote(
            pbuf.at[h, src, part], pbuf.at[h, dst, part], zss.at[way, h, s, w], zrs.at[way, h, s, w],
            right_z if way == 0 else left_z,
        )

    def zsent(way, s, w):
        return s < half - 1 or (s == half - 1 and w == way)

    def arrive(h, s, w):
        for way in range(2):
            if zsent(way, s, w):
                zcopy(way, h, s, w).wait_recv()
                if s + 1 < half and zsent(way, s + 1, w):
                    go(zcopy(way, h, s + 1, w))

    def own(h):
        for w in range(2):
            for way in range(2):
                go(zcopy(way, h, 0, w))

    lo, hi = pl.ds(0, cut), pl.ds(cut, s_ext - cut)
    xc = {
        "ra": remote(ge.at[lo], gx.at[0, lo], xss.at[0], xrs.at[0], right_x),
        "rb": remote(ge.at[hi], gx.at[0, hi], xss.at[1], xrs.at[1], right_x),
        "lb": remote(ge.at[hi], gx.at[1, hi], xss.at[2], xrs.at[2], left_x),
        "la": remote(ge.at[lo], gx.at[1, lo], xss.at[3], xrs.at[3], left_x),
        "fa": remote(gx.at[0, lo], gx.at[2, lo], xss.at[4], xrs.at[4], right_x),
        "fb": remote(gx.at[1, hi], gx.at[2, hi], xss.at[5], xrs.at[5], left_x),
    }

    def encode(t):
        src = ge if t == 0 else gx.at[t - 1]
        ids = src[pl.ds(s_dev, 16), :].astype(jnp.int32)
        m = lax.rem(z + nz - ids // 8, nz)
        code = jnp.where(lax.rem(ids // 2, NX) == x, 2 * m + lax.rem(ids, 2), 255).astype(f32).astype(bf16)
        picks = (
            lax.broadcasted_iota(jnp.int32, (16, 512), 0) == lax.broadcasted_iota(jnp.int32, (16, 512), 1) // 128
        ).astype(f32).astype(bf16)
        codes[...] = lax.dot_general(
            code, picks, (((0,), (0,)), ((), ())), preferred_element_type=f32
        ).astype(bf16)

    def expand(t, part):
        src = ge if t == 0 else gx.at[t - 1]
        if part == 0:
            encode(t)

        @pl.loop(part * s_dev // 64, (part + 1) * s_dev // 64)
        def _(i):
            r = pl.ds(pl.multiple_of(i * 32, 32), 32)
            g = [src[r, pl.ds(128 * k, 128)] for k in range(4)]
            q = [codes[r, pl.ds(128 * k, 128)] for k in range(4)]
            for b in range(2 * nz):
                v = jnp.zeros_like(g[0])
                for k in range(4):
                    v = jnp.where(q[k] == jnp.asarray(b, bf16), g[k], v)
                dense[t, r, pl.ds(128 * b, 128)] = v

    def product(h, t, spans, first):
        total = None
        for lo_m, hi_m in spans:
            depth = (hi_m - lo_m) * 256
            term = jnp.dot(
                dense[t, :, pl.ds(lo_m * 256, depth)], pbuf[h, lo_m:hi_m].reshape(depth, 256),
                preferred_element_type=f32,
            )
            total = term if total is None else total + term
        if not first:
            total = total + acc[h, t]
        acc[h, t] = total

    def ccopy(h, t):
        return remote(csend.at[h, t], crecv.at[h, t], css.at[h, t], crs.at[h, t], other_core)

    def give_core(h, t):
        for yy in range(ny):
            csend[h, t, yy] = acc[h, t, pl.ds(pl.multiple_of(128 * yy + 64 * (1 - c), 64), 64), :].astype(bf16)
        go(ccopy(h, t))

    def both(h, t, yy):
        mine = acc[h, t, pl.ds(pl.multiple_of(128 * yy + 64 * c, 64), 64), :]
        return mine + crecv[h, t, yy].astype(f32)

    top, bottom = pl.ds(0, ny // 2), pl.ds(ny // 2, ny // 2)
    tops, bottoms = range(ny // 2), range(ny // 2, ny)

    def ocopy(h, way):
        part = top if way == 0 else bottom
        return remote(
            xs.at[h, 2, part], xo.at[h, way], oss.at[h, way], ors.at[h, way], right_x if way == 0 else left_x
        )

    def qcopy(h, way, part):
        span = top if part == 0 else bottom
        return remote(
            xs.at[h, 1 - way, span], xr.at[h, way, span], qss.at[h, way, part], qrs.at[h, way, part],
            right_x if way == 0 else left_x,
        )

    def ycopy(h, d):
        return remote(ys.at[h, d - 1], yr.at[h, d - 1], yss.at[h, d - 1], yrs.at[h, d - 1], ydev[d])

    def scopy(h, d):
        cols = pl.ds(256 * h, 256)
        return remote(sy.at[0, :, cols], sy.at[d, :, cols], sss.at[h, d - 1], srs.at[h, d - 1], ydev[d])

    def far(h):
        ccopy(h, 3).wait_recv()
        for yy in range(ny):
            xs[h, 2, yy] = both(h, 3, yy).astype(bf16)
        go(ocopy(h, 0))
        go(ocopy(h, 1))

    def beside(h):
        ccopy(h, 2).wait_recv()
        for yy in bottoms:
            xs[h, 1, yy] = both(h, 2, yy).astype(bf16)
        go(qcopy(h, 0, 1))
        ccopy(h, 1).wait_recv()
        for yy in tops:
            xs[h, 0, yy] = both(h, 1, yy).astype(bf16)
        go(qcopy(h, 1, 0))

    def joined(h):
        ocopy(h, 0).wait_recv()
        for yy in tops:
            xs[h, 1, yy] = (both(h, 2, yy) + xo[h, 0, yy].astype(f32)).astype(bf16)
        go(qcopy(h, 0, 0))
        ocopy(h, 1).wait_recv()
        for yy in bottoms:
            xs[h, 0, yy] = (both(h, 1, yy) + xo[h, 1, yy - ny // 2].astype(f32)).astype(bf16)
        go(qcopy(h, 1, 1))

    def home(h):
        ccopy(h, 0).wait_recv()
        for way in range(2):
            for part in range(2):
                qcopy(h, way, part).wait_recv()
        for yy in range(ny):
            rows[h, yy] = both(h, 0, yy) + xr[h, 0, yy].astype(f32) + xr[h, 1, yy].astype(f32)
        for d in range(1, ny):
            ys[h, d - 1] = rows[h, lax.rem(y + d, ny)].astype(bf16)
            go(ycopy(h, d))

    def finish(h):
        total = rows[h, y]
        for d in range(1, ny):
            ycopy(h, d).wait_recv()
            total = total + yr[h, d - 1].astype(f32)
        cols = pl.ds(256 * h, 256)
        sy[0, :, cols] = total.astype(bf16)
        for d in range(1, ny):
            go(scopy(h, d))

    def pass_a():
        xc["ra"].wait_recv()
        go(xc["fa"])

    def pass_b():
        xc["lb"].wait_recv()
        go(xc["fb"])

    def last(h, t):
        product(h, t, late, False)
        give_core(h, t)

    def first(h, t):
        product(h, t, early, True)

    def samples_here(*names):
        for name in names:
            xc[name].wait_recv()

    lag = 2
    early, late = [(0, 6), (11, nz)], [(6, 11)]
    work = {
        1: [pass_a, pass_b],
        3: [
            lambda: (samples_here("rb"), expand(1, 0)), lambda: expand(1, 1),
            lambda: (samples_here("la"), expand(2, 0)), lambda: expand(2, 1),
        ],
        4: [lambda: None, lambda: None, lambda: (samples_here("fa", "fb"), expand(3, 0)), lambda: expand(3, 1)],
        5: [lambda t=t: first(0, t) for t in (3, 2, 1, 0)],
        7: [lambda: first(1, 3), lambda: first(1, 2), lambda: None, lambda: None]
        + [lambda t=t: last(0, t) for t in (3, 2, 1, 0)],
        8: [lambda: far(0), lambda: beside(0), lambda: first(1, 1), lambda: first(1, 0)],
    }
    for e in range(half + lag):
        todo = list(work.get(e, []))
        parts = [h for h in range(2) if 0 <= e - lag * h < half]
        for h in parts:
            if e == lag * h:
                own(h)
        if e == 0:
            for name in ("ra", "lb", "rb", "la"):
                go(xc[name])
            expand(0, 0)
            expand(0, 1)
        if e == half + lag - 1:
            joined(0)
            home(0)
        for w in range(2):
            for h in parts:
                arrive(h, e - lag * h, w)
                if todo:
                    todo.pop(0)()
        for task in todo:
            task()
    last(1, 3)
    last(1, 2)
    far(1)
    last(1, 1)
    last(1, 0)
    beside(1)
    finish(0)
    joined(1)
    home(1)
    finish(1)

    for h in range(2):
        for d in range(1, ny):
            scopy(h, d).wait_recv()
    cx = [(dx, dc) for dx in range(NX) for dc in range(NC)][1:]
    cxdev = {p: here.at(dx=p[0], dc=p[1]) for p in cx}
    zdev = {d: here.at(dz=d) for d in range(1, nz)}
    right = sy[...].reshape(ny * 64, 512)
    left = sy[:, :, pl.ds(pl.multiple_of(128 * y, 128), 128)].reshape(ny * 64, 128)
    gram[...] = lax.dot_general(left, right, (((0,), (0,)), ((), ())), preferred_element_type=f32)
    copies = []
    for n, (dx, dc) in enumerate(cx):
        at = 64 * lax.rem(c + dc, NC) + 16 * lax.rem(x + dx, NX)
        copies.append(
            remote(
                gram.at[pl.ds(pl.multiple_of(at, 16), 16)], gr.at[n], rss.at[n], rrs.at[n], cxdev[(dx, dc)]
            )
        )
        go(copies[-1])
    part = gram[pl.ds(pl.multiple_of(64 * c + 16 * x, 16), 16), :]
    for n, copy in enumerate(copies):
        copy.wait_recv()
        part = part + gr[n]
    for i in range(4):
        for j in range(4):
            zsend[4 * i + j] = part[4 * i : 4 * i + 4, 128 * j : 128 * j + 128]
    copies = []
    for d in range(1, nz):
        copies.append(
            remote(zsend.at[lax.rem(z + d, nz)], zr.at[d - 1], ess.at[d - 1], ers.at[d - 1], zdev[d])
        )
        go(copies[-1])
    total = zsend[z]
    for d, copy in enumerate(copies):
        copy.wait_recv()
        total = total + zr[d]
    zall[z] = total
    copies = [remote(zall.at[z], zall.at[z], ass.at[d - 1], ars.at[d - 1], zdev[d]) for d in range(1, nz)]
    for copy in copies:
        go(copy)
    for d in range(1, nz):
        remote(
            zall.at[z], zall.at[lax.rem(z + nz - d, nz)], ass.at[d - 1], ars.at[d - 1], zdev[d]
        ).wait_recv()
    xall[x] = zall[...]
    copies = [remote(xall.at[x], xall.at[x], bss.at[d - 1], brs.at[d - 1], here.at(dx=d)) for d in range(1, NX)]
    for copy in copies:
        go(copy)
    for d in range(1, NX):
        remote(
            xall.at[x], xall.at[lax.rem(x + NX - d, NX)], bss.at[d - 1], brs.at[d - 1], here.at(dx=d)
        ).wait_recv()
    yall[y, c] = xall[...]
    copies = [remote(yall.at[y, c], yall.at[y, c], dss.at[d - 1], drs.at[d - 1], ydev[d]) for d in range(1, ny)]
    for copy in copies:
        go(copy)
    other = cxdev[(0, 1)]
    go(remote(yall.at[y, c], yall.at[y, c], fss.at[0], frs.at[0], other))
    for d in range(1, ny):
        from_y = lax.rem(y + ny - d, ny)
        remote(yall.at[y, c], yall.at[from_y, c], dss.at[d - 1], drs.at[d - 1], ydev[d]).wait_recv()
        go(remote(yall.at[from_y, c], yall.at[from_y, c], fss.at[d], frs.at[d], other))
    for d in range(ny):
        from_y = lax.rem(y + ny - d, ny)
        remote(yall.at[y, c], yall.at[from_y, 1 - c], fss.at[d], frs.at[d], other).wait_recv()
    for yy in range(ny):
        for cc in range(NC):
            for xx in range(NX):
                at = 128 * yy + 64 * cc + 16 * xx
                for i in range(4):
                    for j in range(4):
                        whole[at + 4 * i : at + 4 * i + 4, 128 * j : 128 * j + 128] = yall[yy, cc, xx, 4 * i + j]
    width = whole.shape[0]
    diag = lax.broadcasted_iota(jnp.int32, (width, width), 0) == lax.broadcasted_iota(jnp.int32, (width, width), 1)
    g = whole[...]
    g = jnp.where(diag, g + ridge * samples, g)
    scale = jnp.sum(jnp.where(diag, g, 0.0), keepdims=True) * (1.0 / width)
    w = g / scale
    v = sy[0].astype(f32)
    for step in range(root_steps):
        m = jnp.where(diag, 1.5 - 0.5 * w, -0.5 * w)
        mp = pieces(m)
        v = times(pieces(v), mp)
        if step + 1 < root_steps:
            w = times(pieces(times(pieces(w), mp)), mp)
    out[...] = v * (math.sqrt(samples) / jnp.sqrt(scale))
    for copy in started:
        copy.wait_send()


def local(grads, block_ids, probe):
    nz, ny = sizes()
    s_dev = grads.shape[1]
    half = nz // 2
    n = NX * NC - 1
    dma = pltpu.SemaphoreType.DMA
    vmem = pltpu.VMEM
    return pl.pallas_call(
        lambda *refs: kernel(nz, ny, s_dev * nz * NX, *refs),
        out_shape=jax.ShapeDtypeStruct((64, 512), f32),
        in_specs=[pl.BlockSpec(memory_space=pltpu.VMEM)] * 3,
        out_specs=pl.BlockSpec(memory_space=pltpu.VMEM),
        scratch_shapes=[
            vmem((s_dev + 16, 512), bf16),
            vmem((3, s_dev + 16, 512), bf16),
            vmem((s_dev, 512), bf16),
            vmem((4, s_dev, nz * 256), bf16),
            vmem((2, nz, 256, 256), bf16),
            vmem((2, 4, s_dev, 256), f32),
            vmem((2, 4, ny, 64, 256), bf16),
            vmem((2, 4, ny, 64, 256), bf16),
            vmem((2, 3, ny, 64, 256), bf16),
            vmem((2, 2, ny // 2, 64, 256), bf16),
            vmem((2, 2, ny, 64, 256), bf16),
            vmem((2, ny, 64, 256), f32),
            vmem((2, ny - 1, 64, 256), bf16),
            vmem((2, ny - 1, 64, 256), bf16),
            vmem((ny, 64, 512), bf16),
            vmem((128, 512), f32),
            vmem((n, 16, 512), f32),
            vmem((nz, 4, 128), f32),
            vmem((nz - 1, 4, 128), f32),
            vmem((nz, 4, 128), f32),
            vmem((NX, nz, 4, 128), f32),
            vmem((ny, NC, NX, nz, 4, 128), f32),
            vmem((512, 512), f32),
            dma((2, 2, half, 2)), dma((2, 2, half, 2)),
            dma((6,)), dma((6,)),
            dma((2, 4)), dma((2, 4)),
            dma((2, 2)), dma((2, 2)),
            dma((2, 2, 2)), dma((2, 2, 2)),
            dma((2, ny - 1)), dma((2, ny - 1)),
            dma((2, ny - 1)), dma((2, ny - 1)),
            dma((n,)), dma((n,)),
            dma((nz - 1,)), dma((nz - 1,)),
            dma((ny,)), dma((ny,)),
            dma((nz - 1,)), dma((nz - 1,)),
            dma((NX - 1,)), dma((NX - 1,)),
            dma((ny - 1,)), dma((ny - 1,)),
        ],
        compiler_params=pltpu.CompilerParams(
            collective_id=0, has_side_effects=True, vmem_limit_bytes=58 << 20
        ),
        name="whiten",
    )(grads.reshape(s_dev * 4, 128), block_ids[0].T, probe.reshape(256, 512))


def solution(mesh):
    return jax.shard_map(
        local,
        mesh=mesh,
        in_specs=(P("feat", "dp", None, None), P("feat", "dp", None), P("dp", "feat", None, None)),
        out_specs=P(("dp", "feat"), None),
        check_vma=False,
    )
```

```python
import math

import jax
import jax.numpy as jnp
from jax import lax
from jax.experimental import pallas as pl
from jax.experimental.pallas import tpu as pltpu
from jax.sharding import PartitionSpec as P

ridge = 0.1
root_steps = 4
NX = 4
NC = 2
MESH = pl.DeviceIdType.MESH
bf16, f32 = jnp.bfloat16, jnp.float32


def sizes():
    return lax.axis_size("dp") // NX, lax.axis_size("feat") // NC


class Place:
    def __init__(self, nz, ny):
        dp, feat = lax.axis_index("dp"), lax.axis_index("feat")
        self.nz, self.ny = nz, ny
        self.z, self.x = dp // NX, lax.rem(dp, NX)
        self.y, self.c = feat // NC, lax.rem(feat, NC)

    def at(self, dz=0, dx=0, dy=0, dc=0):
        z = lax.rem(self.z + (dz % self.nz), self.nz)
        x = lax.rem(self.x + (dx % NX), NX)
        y = lax.rem(self.y + (dy % self.ny), self.ny)
        c = lax.rem(self.c + dc, NC)
        return {"dp": z * NX + x, "feat": y * NC + c}


def pieces(value):
    hi = value.astype(bf16)
    return hi, (value - hi.astype(f32)).astype(bf16)


def times(a, b):
    (ah, al), (bh, bl) = a, b
    total = jnp.dot(ah, bh, preferred_element_type=f32) + jnp.dot(ah, bl, preferred_element_type=f32)
    return total + jnp.dot(al, bh, preferred_element_type=f32)


def kernel(
    nz, ny, samples, grads, ids, probe, out,
    ge, gx, codes, dense, pbuf, acc, csend, crecv, ps, pr,
    sy, gram, gr, qs, qr, qall, ball, yall, whole,
    zss, zrs, xss, xrs, css, crs, pss, prs,
    sss, srs, rss, rrs, ess, ers, fss, frs, ass, ars, bss, brs, dss, drs,
):
    here = Place(nz, ny)
    z, x, y, c = here.z, here.x, here.y, here.c
    s_dev, s_ext = 512, ge.shape[0]
    cut = 272
    right_z, left_z = here.at(dz=1), here.at(dz=-1)
    right_x, left_x = here.at(dx=1), here.at(dx=-1)
    other_core = here.at(dc=1)
    ydev = {d: here.at(dy=d) for d in range(1, ny)}
    plane = {(dx, dy): here.at(dx=dx, dy=dy) for dx in (2, 1, 3, 0) for dy in range(ny) if (dx, dy) != (0, 0)}
    near = [right_z, left_z, other_core] + list(plane.values())
    barrier = pltpu.get_barrier_semaphore()
    for other in near:
        pl.semaphore_signal(barrier, inc=1, device_id=other, device_id_type=MESH)

    for h in range(2):
        pbuf[h, 0] = probe[:, pl.ds(256 * h, 256)]
    row = lax.broadcasted_iota(jnp.int32, (256, 256), 0)
    picked = 4 * lax.rem(row, 64) + row // 64 == lax.broadcasted_iota(jnp.int32, (256, 256), 1)
    pick = picked.astype(f32).astype(bf16)
    for i in range(s_dev // 64):
        part = jnp.dot(pick, grads[256 * i : 256 * i + 256], preferred_element_type=f32).astype(bf16)
        for k in range(4):
            ge[64 * i : 64 * i + 64, 128 * k : 128 * k + 128] = part[64 * k : 64 * k + 64]
    ge[s_dev:, :] = jnp.concatenate([ids[...].astype(f32), jnp.zeros((12, s_dev), f32)], axis=0).astype(bf16)
    pl.semaphore_wait(barrier, len(near))

    def remote(src, dst, ssem, rsem, to):
        return pltpu.make_async_remote_copy(
            src_ref=src, dst_ref=dst, send_sem=ssem, recv_sem=rsem, device_id=to, device_id_type=MESH
        )

    half = nz // 2
    started = []

    def go(copy):
        copy.start()
        started.append(copy)

    def zcopy(way, h, s, w):
        src, dst = (s, s + 1) if way == 0 else ((nz - s) % nz, nz - 1 - s)
        part = pl.ds(128 * w, 128)
        return remote(
            pbuf.at[h, src, part], pbuf.at[h, dst, part], zss.at[way, h, s, w], zrs.at[way, h, s, w],
            right_z if way == 0 else left_z,
        )

    def zsent(way, s, w):
        return s < half - 1 or (s == half - 1 and w == way)

    def arrive(h, s, w):
        for way in range(2):
            if zsent(way, s, w):
                zcopy(way, h, s, w).wait_recv()
                if s + 1 < half and zsent(way, s + 1, w):
                    go(zcopy(way, h, s + 1, w))

    def own(h):
        for w in range(2):
            for way in range(2):
                go(zcopy(way, h, 0, w))

    lo, hi = pl.ds(0, cut), pl.ds(cut, s_ext - cut)
    xc = {
        "ra": remote(ge.at[lo], gx.at[0, lo], xss.at[0], xrs.at[0], right_x),
        "rb": remote(ge.at[hi], gx.at[0, hi], xss.at[1], xrs.at[1], right_x),
        "lb": remote(ge.at[hi], gx.at[1, hi], xss.at[2], xrs.at[2], left_x),
        "la": remote(ge.at[lo], gx.at[1, lo], xss.at[3], xrs.at[3], left_x),
        "fa": remote(gx.at[0, lo], gx.at[2, lo], xss.at[4], xrs.at[4], right_x),
        "fb": remote(gx.at[1, hi], gx.at[2, hi], xss.at[5], xrs.at[5], left_x),
    }

    def encode(t):
        src = ge if t == 0 else gx.at[t - 1]
        ids = src[pl.ds(s_dev, 16), :].astype(jnp.int32)
        m = lax.rem(z + nz - ids // 8, nz)
        code = jnp.where(lax.rem(ids // 2, NX) == x, 2 * m + lax.rem(ids, 2), 255).astype(f32).astype(bf16)
        picks = (
            lax.broadcasted_iota(jnp.int32, (16, 512), 0) == lax.broadcasted_iota(jnp.int32, (16, 512), 1) // 128
        ).astype(f32).astype(bf16)
        codes[...] = lax.dot_general(
            code, picks, (((0,), (0,)), ((), ())), preferred_element_type=f32
        ).astype(bf16)

    def expand(t, part):
        src = ge if t == 0 else gx.at[t - 1]
        if part == 0:
            encode(t)

        @pl.loop(part * s_dev // 64, (part + 1) * s_dev // 64)
        def _(i):
            r = pl.ds(pl.multiple_of(i * 32, 32), 32)
            g = [src[r, pl.ds(128 * k, 128)] for k in range(4)]
            q = [codes[r, pl.ds(128 * k, 128)] for k in range(4)]
            for b in range(2 * nz):
                v = jnp.zeros_like(g[0])
                for k in range(4):
                    v = jnp.where(q[k] == jnp.asarray(b, bf16), g[k], v)
                dense[t, r, pl.ds(128 * b, 128)] = v

    def product(h, t, spans, first):
        total = None
        for lo_m, hi_m in spans:
            depth = (hi_m - lo_m) * 256
            term = jnp.dot(
                dense[t, :, pl.ds(lo_m * 256, depth)], pbuf[h, lo_m:hi_m].reshape(depth, 256),
                preferred_element_type=f32,
            )
            total = term if total is None else total + term
        if not first:
            total = total + acc[h, t]
        acc[h, t] = total

    def ccopy(h, t):
        return remote(csend.at[h, t], crecv.at[h, t], css.at[h, t], crs.at[h, t], other_core)

    def give_core(h, t):
        for yy in range(ny):
            csend[h, t, yy] = acc[h, t, pl.ds(pl.multiple_of(128 * yy + 64 * (1 - c), 64), 64), :].astype(bf16)
        go(ccopy(h, t))

    def pcopy(h, dx, dy):
        return remote(ps.at[h, dx, dy], pr.at[h, dx, dy], pss.at[h, dx, dy], prs.at[h, dx, dy], plane[(dx, dy)])

    def scopy(h, d):
        cols = pl.ds(256 * h, 256)
        return remote(sy.at[0, :, cols], sy.at[d, :, cols], sss.at[h, d - 1], srs.at[h, d - 1], ydev[d])

    def spread(h, t):
        dx = (0, 3, 1, 2)[t]
        ccopy(h, t).wait_recv()
        for dy in reversed(range(ny)):
            yy = lax.rem(y + dy, ny)
            mine = acc[h, t, pl.ds(pl.multiple_of(128 * yy + 64 * c, 64), 64), :]
            both = mine + crecv[h, t, yy].astype(f32)
            if (dx, dy) == (0, 0):
                acc[h, 0, 0:64] = both
            else:
                ps[h, dx, dy] = both.astype(bf16)
                go(pcopy(h, dx, dy))

    def finish(h):
        total = acc[h, 0, 0:64]
        for dx, dy in plane:
            pcopy(h, dx, dy).wait_recv()
            total = total + pr[h, dx, dy].astype(f32)
        cols = pl.ds(256 * h, 256)
        sy[0, :, cols] = total.astype(bf16)
        for d in range(1, ny):
            go(scopy(h, d))

    def pass_a():
        xc["ra"].wait_recv()
        go(xc["fa"])

    def pass_b():
        xc["lb"].wait_recv()
        go(xc["fb"])

    def last(h, t):
        product(h, t, late, False)
        give_core(h, t)

    def first(h, t):
        product(h, t, early, True)

    def samples_here(*names):
        for name in names:
            xc[name].wait_recv()

    lag = 2
    early, late = [(0, 6), (11, nz)], [(6, 11)]
    work = {
        1: [pass_a, pass_b],
        3: [
            lambda: (samples_here("rb"), expand(1, 0)), lambda: expand(1, 1),
            lambda: (samples_here("la"), expand(2, 0)), lambda: expand(2, 1),
        ],
        4: [lambda: None, lambda: None, lambda: (samples_here("fa", "fb"), expand(3, 0)), lambda: expand(3, 1)],
        5: [lambda t=t: first(0, t) for t in (3, 2, 1, 0)],
        7: [lambda: first(1, 3), lambda: first(1, 2), lambda: None, lambda: None]
        + [lambda t=t: last(0, t) for t in (3, 2, 1, 0)],
        8: [lambda: spread(0, 3), lambda: first(1, 1), lambda: spread(0, 2), lambda: first(1, 0), lambda: (spread(0, 1), spread(0, 0))],
    }
    for e in range(half + lag):
        todo = list(work.get(e, []))
        parts = [h for h in range(2) if 0 <= e - lag * h < half]
        for h in parts:
            if e == lag * h:
                own(h)
        if e == 0:
            for name in ("ra", "lb", "rb", "la"):
                go(xc[name])
            expand(0, 0)
            expand(0, 1)
        for w in range(2):
            for h in parts:
                arrive(h, e - lag * h, w)
                if todo:
                    todo.pop(0)()
        for task in todo:
            task()
    last(1, 3)
    last(1, 2)
    spread(1, 3)
    last(1, 1)
    spread(1, 2)
    last(1, 0)
    spread(1, 1)
    spread(1, 0)
    finish(0)
    finish(1)

    for h in range(2):
        for d in range(1, ny):
            scopy(h, d).wait_recv()
    cx = [(dx, dc) for dx in range(NX) for dc in range(NC)][1:]
    cxdev = {p: here.at(dx=p[0], dc=p[1]) for p in cx}
    right = sy[...].reshape(ny * 64, 512)
    left = sy[:, :, pl.ds(pl.multiple_of(128 * y, 128), 128)].reshape(ny * 64, 128)
    gram[...] = lax.dot_general(left, right, (((0,), (0,)), ((), ())), preferred_element_type=f32)
    copies = []
    for n, (dx, dc) in enumerate(cx):
        at = 64 * lax.rem(c + dc, NC) + 16 * lax.rem(x + dx, NX)
        copies.append(
            remote(
                gram.at[pl.ds(pl.multiple_of(at, 16), 16)], gr.at[n], rss.at[n], rrs.at[n], cxdev[(dx, dc)]
            )
        )
        go(copies[-1])
    part = gram[pl.ds(pl.multiple_of(64 * c + 16 * x, 16), 16), :]
    for n, copy in enumerate(copies):
        copy.wait_recv()
        part = part + gr[n]
    zpart, zat = z // 4, lax.rem(z, 4)
    for i in range(4):
        qs[i] = part[4 * i : 4 * i + 4]

    def zpeer(d):
        return {"dp": (4 * zpart + lax.rem(zat + d, 4)) * NX + x, "feat": y * NC + c}

    copies = []
    for d in range(1, 4):
        copies.append(remote(qs.at[lax.rem(zat + d, 4)], qr.at[d - 1], ess.at[d - 1], ers.at[d - 1], zpeer(d)))
        go(copies[-1])
    total = qs[zat]
    for d, copy in enumerate(copies):
        copy.wait_recv()
        total = total + qr[d]
    parts = nz // 4
    qall[zpart] = total
    for d in range(1, parts):
        go(remote(qall.at[zpart], qall.at[zpart], ass.at[d - 1], ars.at[d - 1], here.at(dz=4 * d)))
    for d in range(1, parts):
        source = lax.rem(zpart + parts - d, parts)
        remote(qall.at[zpart], qall.at[source], ass.at[d - 1], ars.at[d - 1], here.at(dz=4 * d)).wait_recv()
    total = qall[0]
    for i in range(1, parts):
        total = total + qall[i]
    ball[zat] = total
    for d in range(1, 4):
        go(remote(ball.at[zat], ball.at[zat], bss.at[d - 1], brs.at[d - 1], zpeer(d)))
    for d in range(1, 4):
        source = lax.rem(zat + 4 - d, 4)
        remote(ball.at[zat], ball.at[source], bss.at[d - 1], brs.at[d - 1], zpeer(d)).wait_recv()
    yall[c, y, x] = ball[...]
    for dx, dy in plane:
        go(remote(ball, yall.at[c, y, x], dss.at[dx, dy], drs.at[dx, dy], plane[(dx, dy)]))
    for dy in (0, 1, 3, 2):
        from_y = lax.rem(y + ny - dy, ny)
        for dx in range(NX):
            if (dx, dy) != (0, 0):
                from_x = lax.rem(x + NX - dx, NX)
                remote(
                    ball, yall.at[c, from_y, from_x], dss.at[dx, dy], drs.at[dx, dy], plane[(dx, dy)]
                ).wait_recv()
        go(remote(yall.at[c, from_y], yall.at[c, from_y], fss.at[dy], frs.at[dy], other_core))
    for dy in range(ny):
        from_y = lax.rem(y + ny - dy, ny)
        remote(yall.at[c, from_y], yall.at[1 - c, from_y], fss.at[dy], frs.at[dy], other_core).wait_recv()
    for yy in range(ny):
        for cc in range(NC):
            for xx in range(NX):
                at = 128 * yy + 64 * cc + 16 * xx
                for i in range(4):
                    whole[at + 4 * i : at + 4 * i + 4, :] = yall[cc, yy, xx, i]
    width = whole.shape[0]
    diag = lax.broadcasted_iota(jnp.int32, (width, width), 0) == lax.broadcasted_iota(jnp.int32, (width, width), 1)
    g = whole[...]
    g = jnp.where(diag, g + ridge * samples, g)
    scale = jnp.sum(jnp.where(diag, g, 0.0), keepdims=True) * (1.0 / width)
    w = g / scale
    v = sy[0].astype(f32)
    for step in range(root_steps - 1):
        wp = pieces(w)
        mp = pieces(jnp.where(diag, 1.5 - 0.5 * w, -0.5 * w))
        v = times(pieces(v), mp)
        if step + 2 < root_steps:
            w = times(pieces(times(wp, mp)), mp)
    u = times(pieces(times(pieces(times(pieces(v), wp)), mp)), mp)
    v = 1.5 * v - 0.5 * u
    out[...] = v * (math.sqrt(samples) / jnp.sqrt(scale))
    for copy in started:
        copy.wait_send()


def local(grads, block_ids, probe):
    nz, ny = sizes()
    s_dev = grads.shape[1]
    half = nz // 2
    n = NX * NC - 1
    dma = pltpu.SemaphoreType.DMA
    vmem = pltpu.VMEM
    return pl.pallas_call(
        lambda *refs: kernel(nz, ny, s_dev * nz * NX, *refs),
        out_shape=jax.ShapeDtypeStruct((64, 512), f32),
        in_specs=[pl.BlockSpec(memory_space=pltpu.VMEM)] * 3,
        out_specs=pl.BlockSpec(memory_space=pltpu.VMEM),
        scratch_shapes=[
            vmem((s_dev + 16, 512), bf16),
            vmem((3, s_dev + 16, 512), bf16),
            vmem((s_dev, 512), bf16),
            vmem((4, s_dev, nz * 256), bf16),
            vmem((2, nz, 256, 256), bf16),
            vmem((2, 4, s_dev, 256), f32),
            vmem((2, 4, ny, 64, 256), bf16),
            vmem((2, 4, ny, 64, 256), bf16),
            vmem((2, NX, ny, 64, 256), bf16),
            vmem((2, NX, ny, 64, 256), bf16),
            vmem((ny, 64, 512), bf16),
            vmem((128, 512), f32),
            vmem((n, 16, 512), f32),
            vmem((4, 4, 512), f32),
            vmem((3, 4, 512), f32),
            vmem((nz // 4, 4, 512), f32),
            vmem((4, 4, 512), f32),
            vmem((NC, ny, NX, 4, 4, 512), f32),
            vmem((512, 512), f32),
            dma((2, 2, half, 2)), dma((2, 2, half, 2)),
            dma((6,)), dma((6,)),
            dma((2, 4)), dma((2, 4)),
            dma((2, NX, ny)), dma((2, NX, ny)),
            dma((2, ny - 1)), dma((2, ny - 1)),
            dma((n,)), dma((n,)),
            dma((3,)), dma((3,)),
            dma((ny,)), dma((ny,)),
            dma((nz // 4 - 1,)), dma((nz // 4 - 1,)),
            dma((3,)), dma((3,)),
            dma((NX, ny)), dma((NX, ny)),
        ],
        compiler_params=pltpu.CompilerParams(
            collective_id=0, has_side_effects=True, vmem_limit_bytes=58 << 20
        ),
        name="whiten",
    )(grads.reshape(s_dev * 4, 128), block_ids[0].T, probe.reshape(256, 512))


def solution(mesh):
    return jax.shard_map(
        local,
        mesh=mesh,
        in_specs=(P("feat", "dp", None, None), P("feat", "dp", None), P("dp", "feat", None, None)),
        out_specs=P(("dp", "feat"), None),
        check_vma=False,
    )
```

```python
import math

import jax
import jax.numpy as jnp
from jax import lax
from jax.experimental import pallas as pl
from jax.experimental.pallas import tpu as pltpu
from jax.sharding import PartitionSpec as P

ridge = 0.1
root_steps = 4
NX = 4
NC = 2
MESH = pl.DeviceIdType.MESH
bf16, f32 = jnp.bfloat16, jnp.float32


def sizes():
    return lax.axis_size("dp") // NX, lax.axis_size("feat") // NC


class Place:
    def __init__(self, nz, ny):
        dp, feat = lax.axis_index("dp"), lax.axis_index("feat")
        self.nz, self.ny = nz, ny
        self.z, self.x = dp // NX, lax.rem(dp, NX)
        self.y, self.c = feat // NC, lax.rem(feat, NC)

    def at(self, dz=0, dx=0, dy=0, dc=0):
        z = lax.rem(self.z + (dz % self.nz), self.nz)
        x = lax.rem(self.x + (dx % NX), NX)
        y = lax.rem(self.y + (dy % self.ny), self.ny)
        c = lax.rem(self.c + dc, NC)
        return {"dp": z * NX + x, "feat": y * NC + c}


def pieces(value):
    hi = value.astype(bf16)
    return hi, (value - hi.astype(f32)).astype(bf16)


def times(a, b):
    (ah, al), (bh, bl) = a, b
    total = jnp.dot(ah, bh, preferred_element_type=f32) + jnp.dot(ah, bl, preferred_element_type=f32)
    return total + jnp.dot(al, bh, preferred_element_type=f32)


def kernel(
    nz, ny, samples, grads_in, ids_in, probe, out,
    grads, ids, ge, gx, codes, dense, pbuf, acc, csend, crecv, ps, pr,
    sy, gram, gr, qs, qr, qall, ball, yall, whole,
    zss, zrs, xss, xrs, css, crs, pss, prs,
    sss, srs, rss, rrs, ess, ers, fss, frs, ass, ars, bss, brs, dss, drs, ins,
):
    here = Place(nz, ny)
    z, x, y, c = here.z, here.x, here.y, here.c
    s_dev, s_ext = 512, ge.shape[0]
    cut = 272
    right_z, left_z = here.at(dz=1), here.at(dz=-1)
    right_x, left_x = here.at(dx=1), here.at(dx=-1)
    other_core = here.at(dc=1)
    ydev = {d: here.at(dy=d) for d in range(1, ny)}
    plane = {(dx, dy): here.at(dx=dx, dy=dy) for dx in (2, 1, 3, 0) for dy in range(ny) if (dx, dy) != (0, 0)}
    near = [right_z, left_z, other_core] + list(plane.values())
    barrier = pltpu.get_barrier_semaphore()
    for other in near:
        pl.semaphore_signal(barrier, inc=1, device_id=other, device_id_type=MESH)

    fetch = [pltpu.make_async_copy(grads_in, grads, ins.at[0]), pltpu.make_async_copy(ids_in, ids, ins.at[1])]
    fetch += [
        pltpu.make_async_copy(probe.at[:, pl.ds(256 * h, 256)], pbuf.at[h, 0], ins.at[2 + h]) for h in range(2)
    ]
    for copy in fetch:
        copy.start()
    for copy in fetch:
        copy.wait()
    row = lax.broadcasted_iota(jnp.int32, (256, 256), 0)
    picked = 4 * lax.rem(row, 64) + row // 64 == lax.broadcasted_iota(jnp.int32, (256, 256), 1)
    pick = picked.astype(f32).astype(bf16)
    for i in range(s_dev // 64):
        part = jnp.dot(pick, grads[256 * i : 256 * i + 256], preferred_element_type=f32).astype(bf16)
        for k in range(4):
            ge[64 * i : 64 * i + 64, 128 * k : 128 * k + 128] = part[64 * k : 64 * k + 64]
    ge[s_dev:, :] = jnp.concatenate([ids[...].astype(f32), jnp.zeros((12, s_dev), f32)], axis=0).astype(bf16)
    pl.semaphore_wait(barrier, len(near))

    def remote(src, dst, ssem, rsem, to):
        return pltpu.make_async_remote_copy(
            src_ref=src, dst_ref=dst, send_sem=ssem, recv_sem=rsem, device_id=to, device_id_type=MESH
        )

    half = nz // 2
    started = []

    def go(copy):
        copy.start()
        started.append(copy)

    def zcopy(way, h, s, w):
        src, dst = (s, s + 1) if way == 0 else ((nz - s) % nz, nz - 1 - s)
        part = pl.ds(128 * w, 128)
        return remote(
            pbuf.at[h, src, part], pbuf.at[h, dst, part], zss.at[way, h, s, w], zrs.at[way, h, s, w],
            right_z if way == 0 else left_z,
        )

    def zsent(way, s, w):
        return s < half - 1 or (s == half - 1 and w == way)

    def arrive(h, s, w):
        for way in range(2):
            if zsent(way, s, w):
                zcopy(way, h, s, w).wait_recv()
                if s + 1 < half and zsent(way, s + 1, w):
                    go(zcopy(way, h, s + 1, w))

    def own(h):
        for w in range(2):
            for way in range(2):
                go(zcopy(way, h, 0, w))

    lo, hi = pl.ds(0, cut), pl.ds(cut, s_ext - cut)
    xc = {
        "ra": remote(ge.at[lo], gx.at[0, lo], xss.at[0], xrs.at[0], right_x),
        "rb": remote(ge.at[hi], gx.at[0, hi], xss.at[1], xrs.at[1], right_x),
        "lb": remote(ge.at[hi], gx.at[1, hi], xss.at[2], xrs.at[2], left_x),
        "la": remote(ge.at[lo], gx.at[1, lo], xss.at[3], xrs.at[3], left_x),
        "fa": remote(gx.at[0, lo], gx.at[2, lo], xss.at[4], xrs.at[4], right_x),
        "fb": remote(gx.at[1, hi], gx.at[2, hi], xss.at[5], xrs.at[5], left_x),
    }

    def encode(t):
        src = ge if t == 0 else gx.at[t - 1]
        ids = src[pl.ds(s_dev, 16), :].astype(jnp.int32)
        m = lax.rem(z + nz - ids // 8, nz)
        code = jnp.where(lax.rem(ids // 2, NX) == x, 2 * m + lax.rem(ids, 2), 255).astype(f32).astype(bf16)
        picks = (
            lax.broadcasted_iota(jnp.int32, (16, 512), 0) == lax.broadcasted_iota(jnp.int32, (16, 512), 1) // 128
        ).astype(f32).astype(bf16)
        codes[...] = lax.dot_general(
            code, picks, (((0,), (0,)), ((), ())), preferred_element_type=f32
        ).astype(bf16)

    def expand(t, part):
        src = ge if t == 0 else gx.at[t - 1]
        if part == 0:
            encode(t)

        @pl.loop(part * s_dev // 64, (part + 1) * s_dev // 64)
        def _(i):
            r = pl.ds(pl.multiple_of(i * 32, 32), 32)
            g = [src[r, pl.ds(128 * k, 128)] for k in range(4)]
            q = [codes[r, pl.ds(128 * k, 128)] for k in range(4)]
            for b in range(2 * nz):
                v = jnp.zeros_like(g[0])
                for k in range(4):
                    v = jnp.where(q[k] == jnp.asarray(b, bf16), g[k], v)
                dense[t, r, pl.ds(128 * b, 128)] = v

    def product(h, t, spans, first):
        total = None
        for lo_m, hi_m in spans:
            depth = (hi_m - lo_m) * 256
            term = jnp.dot(
                dense[t, :, pl.ds(lo_m * 256, depth)], pbuf[h, lo_m:hi_m].reshape(depth, 256),
                preferred_element_type=f32,
            )
            total = term if total is None else total + term
        if not first:
            total = total + acc[h, t]
        acc[h, t] = total

    def ccopy(h, t):
        return remote(csend.at[h, t], crecv.at[h, t], css.at[h, t], crs.at[h, t], other_core)

    def give_core(h, t):
        for yy in range(ny):
            csend[h, t, yy] = acc[h, t, pl.ds(pl.multiple_of(128 * yy + 64 * (1 - c), 64), 64), :].astype(bf16)
        go(ccopy(h, t))

    def pcopy(h, dx, dy):
        return remote(ps.at[h, dx, dy], pr.at[h, dx, dy], pss.at[h, dx, dy], prs.at[h, dx, dy], plane[(dx, dy)])

    def scopy(h, d):
        cols = pl.ds(256 * h, 256)
        return remote(sy.at[0, :, cols], sy.at[d, :, cols], sss.at[h, d - 1], srs.at[h, d - 1], ydev[d])

    def spread(h, t):
        dx = (0, 3, 1, 2)[t]
        ccopy(h, t).wait_recv()
        for dy in reversed(range(ny)):
            yy = lax.rem(y + dy, ny)
            mine = acc[h, t, pl.ds(pl.multiple_of(128 * yy + 64 * c, 64), 64), :]
            both = mine + crecv[h, t, yy].astype(f32)
            if (dx, dy) == (0, 0):
                acc[h, 0, 0:64] = both
            else:
                ps[h, dx, dy] = both.astype(bf16)
                go(pcopy(h, dx, dy))

    def finish(h):
        total = acc[h, 0, 0:64]
        for dx, dy in plane:
            pcopy(h, dx, dy).wait_recv()
            total = total + pr[h, dx, dy].astype(f32)
        cols = pl.ds(256 * h, 256)
        sy[0, :, cols] = total.astype(bf16)
        for d in range(1, ny):
            go(scopy(h, d))

    def pass_a():
        xc["ra"].wait_recv()
        go(xc["fa"])

    def pass_b():
        xc["lb"].wait_recv()
        go(xc["fb"])

    def last(h, t):
        product(h, t, late, False)
        give_core(h, t)

    def first(h, t):
        product(h, t, early, True)

    def samples_here(*names):
        for name in names:
            xc[name].wait_recv()

    lag = 2
    early, late = [(0, 6), (11, nz)], [(6, 11)]
    work = {
        1: [pass_a, pass_b],
        3: [
            lambda: (samples_here("rb"), expand(1, 0)), lambda: expand(1, 1),
            lambda: (samples_here("la"), expand(2, 0)), lambda: expand(2, 1),
        ],
        4: [lambda: None, lambda: None, lambda: (samples_here("fa", "fb"), expand(3, 0)), lambda: expand(3, 1)],
        5: [lambda t=t: first(0, t) for t in (3, 2, 1, 0)],
        7: [lambda: first(1, 3), lambda: first(1, 2), lambda: None, lambda: None]
        + [lambda t=t: last(0, t) for t in (3, 2, 1, 0)],
        8: [lambda: spread(0, 3), lambda: first(1, 1), lambda: spread(0, 2), lambda: first(1, 0), lambda: (spread(0, 1), spread(0, 0))],
    }
    for e in range(half + lag):
        todo = list(work.get(e, []))
        parts = [h for h in range(2) if 0 <= e - lag * h < half]
        for h in parts:
            if e == lag * h:
                own(h)
        if e == 0:
            for name in ("ra", "lb", "rb", "la"):
                go(xc[name])
            expand(0, 0)
            expand(0, 1)
        for w in range(2):
            for h in parts:
                arrive(h, e - lag * h, w)
                if todo:
                    todo.pop(0)()
        for task in todo:
            task()
    last(1, 3)
    last(1, 2)
    spread(1, 3)
    last(1, 1)
    spread(1, 2)
    last(1, 0)
    spread(1, 1)
    spread(1, 0)
    finish(0)
    finish(1)

    for h in range(2):
        for d in range(1, ny):
            scopy(h, d).wait_recv()
    cx = [(dx, dc) for dx in range(NX) for dc in range(NC)][1:]
    cxdev = {p: here.at(dx=p[0], dc=p[1]) for p in cx}
    def block(r):
        at = pl.multiple_of(128 * lax.rem(y + r, ny), 128)
        return sy[:, :, pl.ds(at, 128)].reshape(ny * 64, 128)

    left = block(0)
    for r in range(3):
        gram[:, pl.ds(128 * r, 128)] = lax.dot_general(
            left, block(r), (((0,), (0,)), ((), ())), preferred_element_type=f32
        )
    copies = []
    for n, (dx, dc) in enumerate(cx):
        at = 64 * lax.rem(c + dc, NC) + 16 * lax.rem(x + dx, NX)
        copies.append(
            remote(
                gram.at[pl.ds(pl.multiple_of(at, 16), 16)], gr.at[n], rss.at[n], rrs.at[n], cxdev[(dx, dc)]
            )
        )
        go(copies[-1])
    part = gram[pl.ds(pl.multiple_of(64 * c + 16 * x, 16), 16), :]
    for n, copy in enumerate(copies):
        copy.wait_recv()
        part = part + gr[n]
    zpart, zat = z // 4, lax.rem(z, 4)
    for i in range(4):
        qs[i] = part[4 * i : 4 * i + 4]

    def zpeer(d):
        return {"dp": (4 * zpart + lax.rem(zat + d, 4)) * NX + x, "feat": y * NC + c}

    copies = []
    for d in range(1, 4):
        copies.append(remote(qs.at[lax.rem(zat + d, 4)], qr.at[d - 1], ess.at[d - 1], ers.at[d - 1], zpeer(d)))
        go(copies[-1])
    total = qs[zat]
    for d, copy in enumerate(copies):
        copy.wait_recv()
        total = total + qr[d]
    parts = nz // 4
    qall[zpart] = total
    for d in range(1, parts):
        go(remote(qall.at[zpart], qall.at[zpart], ass.at[d - 1], ars.at[d - 1], here.at(dz=4 * d)))
    for d in range(1, parts):
        source = lax.rem(zpart + parts - d, parts)
        remote(qall.at[zpart], qall.at[source], ass.at[d - 1], ars.at[d - 1], here.at(dz=4 * d)).wait_recv()
    total = qall[0]
    for i in range(1, parts):
        total = total + qall[i]
    ball[zat] = total
    for d in range(1, 4):
        go(remote(ball.at[zat], ball.at[zat], bss.at[d - 1], brs.at[d - 1], zpeer(d)))
    for d in range(1, 4):
        source = lax.rem(zat + 4 - d, 4)
        remote(ball.at[zat], ball.at[source], bss.at[d - 1], brs.at[d - 1], zpeer(d)).wait_recv()
    yall[c, y, x] = ball[...]
    for dx, dy in plane:
        go(remote(ball, yall.at[c, y, x], dss.at[dx, dy], drs.at[dx, dy], plane[(dx, dy)]))
    for dy in (0, 1, 3, 2):
        from_y = lax.rem(y + ny - dy, ny)
        for dx in range(NX):
            if (dx, dy) != (0, 0):
                from_x = lax.rem(x + NX - dx, NX)
                remote(
                    ball, yall.at[c, from_y, from_x], dss.at[dx, dy], drs.at[dx, dy], plane[(dx, dy)]
                ).wait_recv()
        go(remote(yall.at[c, from_y], yall.at[c, from_y], fss.at[dy], frs.at[dy], other_core))
    for dy in range(ny):
        from_y = lax.rem(y + ny - dy, ny)
        remote(yall.at[c, from_y], yall.at[1 - c, from_y], fss.at[dy], frs.at[dy], other_core).wait_recv()
    for yy in range(ny):
        for cc in range(NC):
            for xx in range(NX):
                at = 128 * yy + 64 * cc + 16 * xx
                for i in range(4):
                    rows = slice(at + 4 * i, at + 4 * i + 4)
                    for r in range(3):
                        to = 128 * ((yy + r) % ny)
                        whole[rows, to : to + 128] = yall[cc, yy, xx, i, :, 128 * r : 128 * r + 128]
    for yy in range(ny):
        a, b = 128 * yy, 128 * ((yy + 3) % ny)
        whole[a : a + 128, b : b + 128] = whole[b : b + 128, a : a + 128].T
    width = whole.shape[0]
    diag = lax.broadcasted_iota(jnp.int32, (width, width), 0) == lax.broadcasted_iota(jnp.int32, (width, width), 1)
    g = whole[...]
    g = jnp.where(diag, g + ridge * samples, g)
    scale = jnp.sum(jnp.where(diag, g, 0.0), keepdims=True) * (1.0 / width)
    w = g / scale
    v = sy[0].astype(f32)
    for step in range(root_steps - 1):
        wp = pieces(w)
        mp = pieces(jnp.where(diag, 1.5 - 0.5 * w, -0.5 * w))
        v = times(pieces(v), mp)
        if step + 2 < root_steps:
            w = times(pieces(times(wp, mp)), mp)
    u = times(pieces(times(pieces(times(pieces(v), wp)), mp)), mp)
    v = 1.5 * v - 0.5 * u
    out[...] = v * (math.sqrt(samples) / jnp.sqrt(scale))
    for copy in started:
        copy.wait_send()


def local(grads, block_ids, probe):
    nz, ny = sizes()
    s_dev = grads.shape[1]
    half = nz // 2
    n = NX * NC - 1
    dma = pltpu.SemaphoreType.DMA
    vmem = pltpu.VMEM
    return pl.pallas_call(
        lambda *refs: kernel(nz, ny, s_dev * nz * NX, *refs),
        out_shape=jax.ShapeDtypeStruct((64, 512), f32),
        in_specs=[pl.BlockSpec(memory_space=pl.ANY)] * 3,
        out_specs=pl.BlockSpec(memory_space=pltpu.VMEM),
        scratch_shapes=[
            vmem((s_dev * 4, 128), bf16),
            vmem((4, s_dev), jnp.int32),
            vmem((s_dev + 16, 512), bf16),
            vmem((3, s_dev + 16, 512), bf16),
            vmem((s_dev, 512), bf16),
            vmem((4, s_dev, nz * 256), bf16),
            vmem((2, nz, 256, 256), bf16),
            vmem((2, 4, s_dev, 256), f32),
            vmem((2, 4, ny, 64, 256), bf16),
            vmem((2, 4, ny, 64, 256), bf16),
            vmem((2, NX, ny, 64, 256), bf16),
            vmem((2, NX, ny, 64, 256), bf16),
            vmem((ny, 64, 512), bf16),
            vmem((128, 384), f32),
            vmem((n, 16, 384), f32),
            vmem((4, 4, 384), f32),
            vmem((3, 4, 384), f32),
            vmem((nz // 4, 4, 384), f32),
            vmem((4, 4, 384), f32),
            vmem((NC, ny, NX, 4, 4, 384), f32),
            vmem((512, 512), f32),
            dma((2, 2, half, 2)), dma((2, 2, half, 2)),
            dma((6,)), dma((6,)),
            dma((2, 4)), dma((2, 4)),
            dma((2, NX, ny)), dma((2, NX, ny)),
            dma((2, ny - 1)), dma((2, ny - 1)),
            dma((n,)), dma((n,)),
            dma((3,)), dma((3,)),
            dma((ny,)), dma((ny,)),
            dma((nz // 4 - 1,)), dma((nz // 4 - 1,)),
            dma((3,)), dma((3,)),
            dma((NX, ny)), dma((NX, ny)),
            dma((4,)),
        ],
        compiler_params=pltpu.CompilerParams(
            collective_id=0, has_side_effects=True, vmem_limit_bytes=58 << 20
        ),
        name="whiten",
    )(grads.reshape(s_dev * 4, 128), block_ids[0].T, probe.reshape(256, 512))


def solution(mesh):
    return jax.shard_map(
        local,
        mesh=mesh,
        in_specs=(P("feat", "dp", None, None), P("feat", "dp", None), P("dp", "feat", None, None)),
        out_specs=P(("dp", "feat"), None),
        check_vma=False,
    )
```

```python
import math

import jax
import jax.numpy as jnp
from jax import lax
from jax.experimental import pallas as pl
from jax.experimental.pallas import tpu as pltpu
from jax.sharding import PartitionSpec as P

ridge = 0.1
root_steps = 4
NX = 4
NC = 2
MESH = pl.DeviceIdType.MESH
bf16, f32 = jnp.bfloat16, jnp.float32


def sizes():
    return lax.axis_size("dp") // NX, lax.axis_size("feat") // NC


class Place:
    def __init__(self, nz, ny):
        dp, feat = lax.axis_index("dp"), lax.axis_index("feat")
        self.nz, self.ny = nz, ny
        self.z, self.x = dp // NX, lax.rem(dp, NX)
        self.y, self.c = feat // NC, lax.rem(feat, NC)

    def at(self, dz=0, dx=0, dy=0, dc=0):
        z = lax.rem(self.z + (dz % self.nz), self.nz)
        x = lax.rem(self.x + (dx % NX), NX)
        y = lax.rem(self.y + (dy % self.ny), self.ny)
        c = lax.rem(self.c + dc, NC)
        return {"dp": z * NX + x, "feat": y * NC + c}


def pieces(value):
    hi = value.astype(bf16)
    return hi, (value - hi.astype(f32)).astype(bf16)


def times(a, b):
    (ah, al), (bh, bl) = a, b
    total = jnp.dot(ah, bh, preferred_element_type=f32) + jnp.dot(ah, bl, preferred_element_type=f32)
    return total + jnp.dot(al, bh, preferred_element_type=f32)


def kernel(
    nz, ny, samples, grads_in, ids_in, probe, out,
    grads, ids, ge, gx, codes, dense, pbuf, acc, csend, crecv, ps, pr,
    sy, gram, gr, qs, qr, qall, ball, yall, whole,
    zss, zrs, xss, xrs, css, crs, pss, prs,
    sss, srs, rss, rrs, ess, ers, fss, frs, ass, ars, bss, brs, dss, drs, ins,
):
    here = Place(nz, ny)
    z, x, y, c = here.z, here.x, here.y, here.c
    s_dev, s_ext = 512, ge.shape[0]
    cut = 272
    right_z, left_z = here.at(dz=1), here.at(dz=-1)
    right_x, left_x = here.at(dx=1), here.at(dx=-1)
    other_core = here.at(dc=1)
    ydev = {d: here.at(dy=d) for d in range(1, ny)}
    plane = {(dx, dy): here.at(dx=dx, dy=dy) for dx in (2, 1, 3, 0) for dy in range(ny) if (dx, dy) != (0, 0)}
    near = [right_z, left_z, other_core] + list(plane.values())
    barrier = pltpu.get_barrier_semaphore()
    for other in near:
        pl.semaphore_signal(barrier, inc=1, device_id=other, device_id_type=MESH)

    fetch = [pltpu.make_async_copy(grads_in, grads, ins.at[0]), pltpu.make_async_copy(ids_in, ids, ins.at[1])]
    fetch += [
        pltpu.make_async_copy(probe.at[:, pl.ds(256 * h, 256)], pbuf.at[h, 0], ins.at[2 + h]) for h in range(2)
    ]
    for copy in fetch:
        copy.start()
    for copy in fetch:
        copy.wait()
    row = lax.broadcasted_iota(jnp.int32, (256, 256), 0)
    picked = 4 * lax.rem(row, 64) + row // 64 == lax.broadcasted_iota(jnp.int32, (256, 256), 1)
    pick = picked.astype(f32).astype(bf16)
    for i in range(s_dev // 64):
        part = jnp.dot(pick, grads[256 * i : 256 * i + 256], preferred_element_type=f32).astype(bf16)
        for k in range(4):
            ge[64 * i : 64 * i + 64, 128 * k : 128 * k + 128] = part[64 * k : 64 * k + 64]
    ge[s_dev:, :] = jnp.concatenate([ids[...].astype(f32), jnp.zeros((12, s_dev), f32)], axis=0).astype(bf16)
    pl.semaphore_wait(barrier, len(near))

    def remote(src, dst, ssem, rsem, to):
        return pltpu.make_async_remote_copy(
            src_ref=src, dst_ref=dst, send_sem=ssem, recv_sem=rsem, device_id=to, device_id_type=MESH
        )

    half = nz // 2
    started = []

    def go(copy):
        copy.start()
        started.append(copy)

    def zcopy(way, h, s, w):
        src, dst = (s, s + 1) if way == 0 else ((nz - s) % nz, nz - 1 - s)
        part = pl.ds(128 * w, 128)
        return remote(
            pbuf.at[h, src, part], pbuf.at[h, dst, part], zss.at[way, h, s, w], zrs.at[way, h, s, w],
            right_z if way == 0 else left_z,
        )

    def zsent(way, s, w):
        return s < half - 1 or (s == half - 1 and w == way)

    def arrive(h, s, w):
        for way in range(2):
            if zsent(way, s, w):
                zcopy(way, h, s, w).wait_recv()
                if s + 1 < half and zsent(way, s + 1, w):
                    go(zcopy(way, h, s + 1, w))

    def own(h):
        for w in range(2):
            for way in range(2):
                go(zcopy(way, h, 0, w))

    lo, hi = pl.ds(0, cut), pl.ds(cut, s_ext - cut)
    xc = {
        "ra": remote(ge.at[lo], gx.at[0, lo], xss.at[0], xrs.at[0], right_x),
        "rb": remote(ge.at[hi], gx.at[0, hi], xss.at[1], xrs.at[1], right_x),
        "lb": remote(ge.at[hi], gx.at[1, hi], xss.at[2], xrs.at[2], left_x),
        "la": remote(ge.at[lo], gx.at[1, lo], xss.at[3], xrs.at[3], left_x),
        "fa": remote(gx.at[0, lo], gx.at[2, lo], xss.at[4], xrs.at[4], right_x),
        "fb": remote(gx.at[1, hi], gx.at[2, hi], xss.at[5], xrs.at[5], left_x),
    }

    def encode(t):
        src = ge if t == 0 else gx.at[t - 1]
        ids = src[pl.ds(s_dev, 16), :].astype(jnp.int32)
        m = lax.rem(z + nz - ids // 8, nz)
        code = jnp.where(lax.rem(ids // 2, NX) == x, 2 * m + lax.rem(ids, 2), 255).astype(f32).astype(bf16)
        picks = (
            lax.broadcasted_iota(jnp.int32, (16, 512), 0) == lax.broadcasted_iota(jnp.int32, (16, 512), 1) // 128
        ).astype(f32).astype(bf16)
        codes[...] = lax.dot_general(
            code, picks, (((0,), (0,)), ((), ())), preferred_element_type=f32
        ).astype(bf16)

    def expand(t, part):
        src = ge if t == 0 else gx.at[t - 1]
        if part == 0:
            encode(t)

        @pl.loop(part * s_dev // 64, (part + 1) * s_dev // 64)
        def _(i):
            r = pl.ds(pl.multiple_of(i * 32, 32), 32)
            g = [src[r, pl.ds(128 * k, 128)] for k in range(4)]
            q = [codes[r, pl.ds(128 * k, 128)] for k in range(4)]
            for b in range(2 * nz):
                v = jnp.zeros_like(g[0])
                for k in range(4):
                    v = jnp.where(q[k] == jnp.asarray(b, bf16), g[k], v)
                dense[t, r, pl.ds(128 * b, 128)] = v

    def product(h, t, spans, first):
        total = None
        for lo_m, hi_m in spans:
            depth = (hi_m - lo_m) * 256
            term = jnp.dot(
                dense[t, :, pl.ds(lo_m * 256, depth)], pbuf[h, lo_m:hi_m].reshape(depth, 256),
                preferred_element_type=f32,
            )
            total = term if total is None else total + term
        if not first:
            total = total + acc[h, t]
        acc[h, t] = total

    def ccopy(h, t):
        return remote(csend.at[h, t], crecv.at[h, t], css.at[h, t], crs.at[h, t], other_core)

    def give_core(h, t):
        for yy in range(ny):
            csend[h, t, yy] = acc[h, t, pl.ds(pl.multiple_of(128 * yy + 64 * (1 - c), 64), 64), :].astype(bf16)
        go(ccopy(h, t))

    def pcopy(h, dx, dy):
        return remote(ps.at[h, dx, dy], pr.at[h, dx, dy], pss.at[h, dx, dy], prs.at[h, dx, dy], plane[(dx, dy)])

    def scopy(h, d):
        cols = pl.ds(256 * h, 256)
        return remote(sy.at[0, :, cols], sy.at[d, :, cols], sss.at[h, d - 1], srs.at[h, d - 1], ydev[d])

    def spread(h, t):
        dx = (0, 3, 1, 2)[t]
        ccopy(h, t).wait_recv()
        for dy in reversed(range(ny)):
            yy = lax.rem(y + dy, ny)
            mine = acc[h, t, pl.ds(pl.multiple_of(128 * yy + 64 * c, 64), 64), :]
            both = mine + crecv[h, t, yy].astype(f32)
            if (dx, dy) == (0, 0):
                acc[h, 0, 0:64] = both
            else:
                ps[h, dx, dy] = both.astype(bf16)
                go(pcopy(h, dx, dy))

    def finish(h):
        total = acc[h, 0, 0:64]
        for dx, dy in plane:
            pcopy(h, dx, dy).wait_recv()
            total = total + pr[h, dx, dy].astype(f32)
        cols = pl.ds(256 * h, 256)
        sy[0, :, cols] = total.astype(bf16)
        for d in range(1, ny):
            go(scopy(h, d))

    def pass_a():
        xc["ra"].wait_recv()
        go(xc["fa"])

    def pass_b():
        xc["lb"].wait_recv()
        go(xc["fb"])

    def last(h, t):
        product(h, t, end if h else late, False)
        give_core(h, t)

    def first(h, t):
        product(h, t, early, True)

    def samples_here(*names):
        for name in names:
            xc[name].wait_recv()

    lag = 2
    early, late = [(0, 6), (11, nz)], [(6, 11)]
    mid, end = [(6, 8), (9, 11)], [(8, 9)]
    work = {
        1: [pass_a, pass_b],
        3: [
            lambda: (samples_here("rb"), expand(1, 0)), lambda: expand(1, 1),
            lambda: (samples_here("la"), expand(2, 0)), lambda: expand(2, 1),
        ],
        4: [lambda: None, lambda: None, lambda: (samples_here("fa", "fb"), expand(3, 0)), lambda: expand(3, 1)],
        5: [lambda t=t: first(0, t) for t in (3, 2, 1, 0)],
        7: [lambda: first(1, 3), lambda: first(1, 2), lambda: None, lambda: None]
        + [lambda t=t: last(0, t) for t in (3, 2, 1, 0)],
        8: [lambda: spread(0, 3), lambda: first(1, 1), lambda: spread(0, 2), lambda: first(1, 0), lambda: (spread(0, 1), spread(0, 0))],
    }
    for e in range(half + lag):
        todo = list(work.get(e, []))
        parts = [h for h in range(2) if 0 <= e - lag * h < half]
        for h in parts:
            if e == lag * h:
                own(h)
        if e == 0:
            for name in ("ra", "lb", "rb", "la"):
                go(xc[name])
            expand(0, 0)
            expand(0, 1)
        if e == half + lag - 1:
            for t in (3, 2, 1, 0):
                product(1, t, mid, False)
        for w in range(2):
            for h in parts:
                arrive(h, e - lag * h, w)
                if todo:
                    todo.pop(0)()
        for task in todo:
            task()
    last(1, 3)
    last(1, 2)
    spread(1, 3)
    last(1, 1)
    spread(1, 2)
    last(1, 0)
    spread(1, 1)
    spread(1, 0)
    finish(0)
    finish(1)

    for h in range(2):
        for d in range(1, ny):
            scopy(h, d).wait_recv()
    cx = [(dx, dc) for dx in range(NX) for dc in range(NC)][1:]
    cxdev = {p: here.at(dx=p[0], dc=p[1]) for p in cx}
    def block(r):
        at = pl.multiple_of(128 * lax.rem(y + r, ny), 128)
        return sy[:, :, pl.ds(at, 128)].reshape(ny * 64, 128)

    left = block(0)
    for r in range(3):
        gram[:, pl.ds(128 * r, 128)] = lax.dot_general(
            left, block(r), (((0,), (0,)), ((), ())), preferred_element_type=f32
        )
    copies = []
    for n, (dx, dc) in enumerate(cx):
        at = 64 * lax.rem(c + dc, NC) + 16 * lax.rem(x + dx, NX)
        copies.append(
            remote(
                gram.at[pl.ds(pl.multiple_of(at, 16), 16)], gr.at[n], rss.at[n], rrs.at[n], cxdev[(dx, dc)]
            )
        )
        go(copies[-1])
    part = gram[pl.ds(pl.multiple_of(64 * c + 16 * x, 16), 16), :]
    for n, copy in enumerate(copies):
        copy.wait_recv()
        part = part + gr[n]
    zpart, zat = z // 4, lax.rem(z, 4)
    for i in range(4):
        qs[i] = part[4 * i : 4 * i + 4]

    def zpeer(d):
        return {"dp": (4 * zpart + lax.rem(zat + d, 4)) * NX + x, "feat": y * NC + c}

    copies = []
    for d in range(1, 4):
        copies.append(remote(qs.at[lax.rem(zat + d, 4)], qr.at[d - 1], ess.at[d - 1], ers.at[d - 1], zpeer(d)))
        go(copies[-1])
    total = qs[zat]
    for d, copy in enumerate(copies):
        copy.wait_recv()
        total = total + qr[d]
    parts = nz // 4
    qall[zpart] = total
    for d in range(1, parts):
        go(remote(qall.at[zpart], qall.at[zpart], ass.at[d - 1], ars.at[d - 1], here.at(dz=4 * d)))
    for d in range(1, parts):
        source = lax.rem(zpart + parts - d, parts)
        remote(qall.at[zpart], qall.at[source], ass.at[d - 1], ars.at[d - 1], here.at(dz=4 * d)).wait_recv()
    total = qall[0]
    for i in range(1, parts):
        total = total + qall[i]
    ball[zat] = total
    for d in range(1, 4):
        go(remote(ball.at[zat], ball.at[zat], bss.at[d - 1], brs.at[d - 1], zpeer(d)))
    for d in range(1, 4):
        source = lax.rem(zat + 4 - d, 4)
        remote(ball.at[zat], ball.at[source], bss.at[d - 1], brs.at[d - 1], zpeer(d)).wait_recv()
    yall[c, y, x] = ball[...]
    for dx, dy in plane:
        go(remote(ball, yall.at[c, y, x], dss.at[dx, dy], drs.at[dx, dy], plane[(dx, dy)]))
    for dy in (0, 1, 3, 2):
        from_y = lax.rem(y + ny - dy, ny)
        for dx in range(NX):
            if (dx, dy) != (0, 0):
                from_x = lax.rem(x + NX - dx, NX)
                remote(
                    ball, yall.at[c, from_y, from_x], dss.at[dx, dy], drs.at[dx, dy], plane[(dx, dy)]
                ).wait_recv()
        go(remote(yall.at[c, from_y], yall.at[c, from_y], fss.at[dy], frs.at[dy], other_core))
    for dy in range(ny):
        from_y = lax.rem(y + ny - dy, ny)
        remote(yall.at[c, from_y], yall.at[1 - c, from_y], fss.at[dy], frs.at[dy], other_core).wait_recv()
    for yy in range(ny):
        for cc in range(NC):
            for xx in range(NX):
                at = 128 * yy + 64 * cc + 16 * xx
                for i in range(4):
                    rows = slice(at + 4 * i, at + 4 * i + 4)
                    for r in range(3):
                        to = 128 * ((yy + r) % ny)
                        whole[rows, to : to + 128] = yall[cc, yy, xx, i, :, 128 * r : 128 * r + 128]
    for yy in range(ny):
        a, b = 128 * yy, 128 * ((yy + 3) % ny)
        whole[a : a + 128, b : b + 128] = whole[b : b + 128, a : a + 128].T
    width = whole.shape[0]
    diag = lax.broadcasted_iota(jnp.int32, (width, width), 0) == lax.broadcasted_iota(jnp.int32, (width, width), 1)
    g = whole[...]
    g = jnp.where(diag, g + ridge * samples, g)
    scale = jnp.sum(jnp.where(diag, g, 0.0), keepdims=True) * (1.0 / width)
    w = g / scale
    v = sy[0].astype(f32)
    for step in range(root_steps - 1):
        wp = pieces(w)
        mp = pieces(jnp.where(diag, 1.5 - 0.5 * w, -0.5 * w))
        v = times(pieces(v), mp)
        if step + 2 < root_steps:
            w = times(pieces(times(wp, mp)), mp)
    u = times(pieces(times(pieces(times(pieces(v), wp)), mp)), mp)
    v = 1.5 * v - 0.5 * u
    out[...] = v * (math.sqrt(samples) / jnp.sqrt(scale))
    for copy in started:
        copy.wait_send()


def local(grads, block_ids, probe):
    nz, ny = sizes()
    s_dev = grads.shape[1]
    half = nz // 2
    n = NX * NC - 1
    dma = pltpu.SemaphoreType.DMA
    vmem = pltpu.VMEM
    return pl.pallas_call(
        lambda *refs: kernel(nz, ny, s_dev * nz * NX, *refs),
        out_shape=jax.ShapeDtypeStruct((64, 512), f32),
        in_specs=[pl.BlockSpec(memory_space=pl.ANY)] * 3,
        out_specs=pl.BlockSpec(memory_space=pltpu.VMEM),
        scratch_shapes=[
            vmem((s_dev * 4, 128), bf16),
            vmem((4, s_dev), jnp.int32),
            vmem((s_dev + 16, 512), bf16),
            vmem((3, s_dev + 16, 512), bf16),
            vmem((s_dev, 512), bf16),
            vmem((4, s_dev, nz * 256), bf16),
            vmem((2, nz, 256, 256), bf16),
            vmem((2, 4, s_dev, 256), f32),
            vmem((2, 4, ny, 64, 256), bf16),
            vmem((2, 4, ny, 64, 256), bf16),
            vmem((2, NX, ny, 64, 256), bf16),
            vmem((2, NX, ny, 64, 256), bf16),
            vmem((ny, 64, 512), bf16),
            vmem((128, 384), f32),
            vmem((n, 16, 384), f32),
            vmem((4, 4, 384), f32),
            vmem((3, 4, 384), f32),
            vmem((nz // 4, 4, 384), f32),
            vmem((4, 4, 384), f32),
            vmem((NC, ny, NX, 4, 4, 384), f32),
            vmem((512, 512), f32),
            dma((2, 2, half, 2)), dma((2, 2, half, 2)),
            dma((6,)), dma((6,)),
            dma((2, 4)), dma((2, 4)),
            dma((2, NX, ny)), dma((2, NX, ny)),
            dma((2, ny - 1)), dma((2, ny - 1)),
            dma((n,)), dma((n,)),
            dma((3,)), dma((3,)),
            dma((ny,)), dma((ny,)),
            dma((nz // 4 - 1,)), dma((nz // 4 - 1,)),
            dma((3,)), dma((3,)),
            dma((NX, ny)), dma((NX, ny)),
            dma((4,)),
        ],
        compiler_params=pltpu.CompilerParams(
            collective_id=0, has_side_effects=True, vmem_limit_bytes=58 << 20
        ),
        name="whiten",
    )(grads.reshape(s_dev * 4, 128), block_ids[0].T, probe.reshape(256, 512))


def solution(mesh):
    return jax.shard_map(
        local,
        mesh=mesh,
        in_specs=(P("feat", "dp", None, None), P("feat", "dp", None), P("dp", "feat", None, None)),
        out_specs=P(("dp", "feat"), None),
        check_vma=False,
    )
```
